32 devices in a mesh: mass: 8 (over z, y), prot: 4 (over x, core).
Axes of the slice: x: 2, y: 2, z: 4, core: 2. Of those that a mesh axis runs over, the one named last changes fastest.
Arguments:
- spectra: bfloat16 [32768, 512], P(('mass', 'prot')), may hold values from -6 to 6
- peptides: bfloat16 [32768, 512], P(('mass', 'prot')), may hold values from -6 to 6
- destination: int32 [32768], P(('mass', 'prot')), may hold values from 0 to 32767, as said below
- band: int32 [128, 6], P(('mass', 'prot')), may hold values from 0 to 7, as said below
- positive: int32 [32768], P(('mass', 'prot')), may hold values from 0 to 1535
- logit_scale: float32 [1], replicated, may hold values from 1 to 2
- logit_bias: float32 [1], replicated, may hold values from -3 to -1
Outputs:
- spectra_grad: bfloat16 [32768, 512], P(('mass', 'prot'))
- peptide_grad: bfloat16 [32768, 512], P(('mass', 'prot'))
The draws below stay inside these ranges and needn't reach their ends.
Inputs may be any that keep to these rules, and one draw needn't show every extreme that they name: destination is a permutation. A peptide of device s fills a row of the block of 1024 table rows of some device o with the same placement; every device sends between 1 and 63 peptides to every device, and exactly 63 to some in every draw. `band`: the 6 entries of a row are distinct. The first device's blocks never name entries below 2, the last device's never entries at or above 6.
All inputs are finite; a program needn't handle non-finite values.
Results may differ from the reference program's by a relative error of at most 0.0065.
Values may be sent and summed in bfloat16 or wider, within the bound.
No kernel may reach another device: no remote copies, remote signals or barrier semaphores. Data moves between devices by JAX's collectives and lax.ppermute only.
A program may use at most 64 MiB of HBM per device.

```python
import math
import jax
import jax.numpy as jnp
from jax import lax

D = 512
TILE_ROWS = 256
EDGE = 2
NB = 6
TILE_DEV = 4
SB = 4
PEP_DEV = 1024
NTILES = 128
NPEP = 32768
NSPEC = 32768
N_MASS = 8
N_PROT = 4


def pair_counts(key):
    devices = N_MASS * N_PROT
    mean_rows = PEP_DEV // devices
    half = devices // 2
    spread = jax.random.randint(jax.random.fold_in(key, 1), (half,), 0, mean_rows)
    spread = spread.at[0].set(mean_rows - 1)
    deltas = jnp.concatenate([spread, -spread])
    shuffle = jax.random.permutation(jax.random.fold_in(key, 2), devices)
    return (mean_rows + deltas[shuffle]).astype(jnp.int32)


def draw_destination(key, part):
    devices = N_MASS * N_PROT
    rows = PEP_DEV
    counts = pair_counts(jax.random.fold_in(key, 11))
    starts = jnp.cumsum(counts) - counts
    offsets = jnp.repeat(jnp.arange(devices, dtype=jnp.int32), counts, total_repeat_length=rows)
    within = jnp.arange(rows, dtype=jnp.int32) - starts[offsets]
    source = jnp.arange(devices, dtype=jnp.int32)
    matrix = counts[(source[None, :] - source[:, None]) % devices]
    base = jnp.cumsum(matrix, axis=0) - matrix
    row_keys = jax.random.split(jax.random.fold_in(key, 12), devices)
    perms = jax.vmap(lambda k: jax.random.permutation(k, rows))(row_keys)
    picked_off = offsets[perms]
    picked_rank = within[perms]
    owners = (source[:, None] + picked_off) % devices
    base_pick = base[source[:, None], owners]
    owner_keys = jax.random.split(jax.random.fold_in(key, 13), devices)
    owner_perm = jax.vmap(lambda k: jax.random.permutation(k, rows))(owner_keys)
    slots = owner_perm[owners, base_pick + picked_rank]
    return (owners * rows + slots).reshape(devices * rows).astype(jnp.int32)


def draw_band(key, part):
    devices = N_MASS * N_PROT
    ext_count = TILE_DEV + 2 * EDGE
    blocks = devices * SB
    block_keys = jax.random.split(jax.random.fold_in(key, 21), blocks)
    scores = jax.vmap(lambda k: jax.random.permutation(k, ext_count))(block_keys).astype(jnp.int32)
    block_ids = jnp.arange(blocks, dtype=jnp.int32)
    device = block_ids // SB
    first_block = block_ids % SB == 0
    tile_ids = jnp.arange(ext_count, dtype=jnp.int32)
    lower = tile_ids < EDGE
    upper = tile_ids >= ext_count - EDGE
    forced = first_block[:, None] & ((tile_ids == 0) | (tile_ids == ext_count - 1))[None, :]
    banned = (device == 0)[:, None] & lower[None, :] | (device == devices - 1)[:, None] & upper[None, :]
    total = scores + forced.astype(jnp.int32) * (2 * ext_count) - banned.astype(jnp.int32) * (4 * ext_count)
    values, chosen = lax.top_k(total, NB)
    return chosen.astype(jnp.int32)


def plant(array, key, smallest, largest):
    index_at = [jax.random.randint(jax.random.fold_in(key, axis), (), 0, length) for axis, length in enumerate(array.shape)]
    longest = array.shape.index(max(array.shape))
    beside = index_at[:longest] + [(index_at[longest] + 1) % array.shape[longest]] + index_at[longest + 1:]
    return array.at[tuple(index_at)].set(smallest).at[tuple(beside)].set(largest)


def steps_of(key, dims, cuts, low, top_value):
    factor_of = 1.0
    for dim, parts in cuts:
        steps = jax.random.uniform(jax.random.fold_in(jax.random.fold_in(key, 6), dim), (parts,), jnp.float32, low / len(cuts), top_value / len(cuts))
        factor_of = factor_of * jnp.repeat(jnp.exp(steps), dims[dim] // parts).reshape((-1,) + (1,) * (len(dims) - 1 - dim))
    return factor_of


def normal_values(key, extent, scale, most, pieces=(), kind=jnp.bfloat16):
    gain = steps_of(key, extent, pieces, -0.22, 0.18) if pieces else 1.0
    entries = jax.random.normal(key, extent, jnp.float32) * scale * gain
    return jnp.minimum(jnp.maximum(entries, -most), most).astype(kind)


def setup_inputs(seed: int = 0) -> dict:
    streams_of = jax.random.split(jax.random.key(seed), 8)
    return {
        "spectra": normal_values(streams_of[0], (NSPEC, D), 1.0, 6.0, ((0, 32),)),
        "peptides": normal_values(streams_of[1], (NPEP, D), 1.0, 6.0, ((0, 32),)),
        "destination": draw_destination(jax.random.fold_in(streams_of[7], 71), 0),
        "band": draw_band(jax.random.fold_in(streams_of[7], 71), 0),
        "positive": plant(jax.random.randint(streams_of[4], (NSPEC,), 0, NB * TILE_ROWS), jax.random.fold_in(streams_of[4], 1), 0, (NB * TILE_ROWS) - 1).astype(jnp.int32),
        "logit_scale": jnp.clip(jax.random.uniform(streams_of[5], (1,), jnp.float32, 1.0, 2.0), 1.0, 2.0),
        "logit_bias": jnp.clip(jax.random.uniform(streams_of[6], (1,), jnp.float32, -3.0, -1.0), -3.0, -1.0),
    }


def reference(spectra, peptides, destination, band, positive, logit_scale, logit_bias):
    devices = N_MASS * N_PROT
    width = D
    ext_count = TILE_DEV + 2 * EDGE
    table = jnp.zeros_like(peptides).at[destination].set(peptides)
    padded = jnp.pad(table.reshape(NTILES, TILE_ROWS, width), ((EDGE, EDGE), (0, 0), (0, 0)))
    scaling = logit_scale[0] / math.sqrt(width)
    offset = logit_bias[0]
    column_ids = jnp.arange(NB * TILE_ROWS, dtype=jnp.int32)
    spec_all = spectra.reshape(devices, SB, TILE_ROWS, width)
    band_all = band.reshape(devices, SB, NB)
    pos_all = positive.reshape(devices, SB, TILE_ROWS)

    def per_device(grad_pad, inputs):
        device, spec_dev, band_dev, pos_dev = inputs
        begin = device * TILE_DEV
        extended = lax.dynamic_slice_in_dim(padded, begin, ext_count, 0).astype(jnp.float32)
        ext_grad = jnp.zeros((ext_count, TILE_ROWS, width), jnp.float32)
        results = []
        for block in range(SB):
            chosen = band_dev[block]
            columns = extended[chosen].reshape(NB * TILE_ROWS, width)
            spec_block = spec_dev[block].astype(jnp.float32)
            logits = scaling * jnp.dot(spec_block, columns.T, precision=lax.Precision.HIGHEST) + offset
            labels = (column_ids[None, :] == pos_dev[block][:, None]).astype(jnp.float32)
            weights = (jax.nn.sigmoid(logits) - labels).astype(jnp.bfloat16)
            weights = lax.optimization_barrier(weights).astype(jnp.float32)
            spec_grad = scaling * jnp.dot(weights, columns, precision=lax.Precision.HIGHEST)
            results.append(spec_grad.astype(jnp.bfloat16))
            tile_grad = scaling * jnp.dot(weights.T, spec_block, precision=lax.Precision.HIGHEST)
            ext_grad = ext_grad.at[chosen].add(tile_grad.reshape(NB, TILE_ROWS, width))
        window = lax.dynamic_slice_in_dim(grad_pad, begin, ext_count, 0)
        grad_pad = lax.dynamic_update_slice_in_dim(grad_pad, window + ext_grad, begin, 0)
        return (grad_pad, jnp.stack(results))
    grad_start = jnp.zeros((NTILES + 2 * EDGE, TILE_ROWS, width), jnp.float32)
    device_ids = jnp.arange(devices, dtype=jnp.int32)
    grad_pad, spec_grads = lax.scan(per_device, grad_start, (device_ids, spec_all, band_all, pos_all))
    own_grad = grad_pad[EDGE:EDGE + NTILES].reshape(NPEP, width).astype(jnp.bfloat16)
    return (spec_grads.reshape(NSPEC, width), own_grad[destination])
```

```python
import functools
import math

import jax
import jax.numpy as jnp
from jax import lax
from jax.experimental import pallas as pl
from jax.experimental.pallas import tpu as pltpu
from jax.sharding import PartitionSpec as P

TILE_ROWS = 256
EDGE = 2
NB = 6
TILE_DEV = 4
SB = 4
CHUNK = 256
AXES = ("mass", "prot")
BASE = 256


def log2(value):
    bits = value.bit_length() - 1
    assert value == 1 << bits
    return bits


def iota(shape, dim):
    return lax.broadcasted_iota(jnp.int32, shape, dim)


def onehot(mask):
    return jnp.where(mask, 1.0, 0.0).astype(jnp.bfloat16)


def matmul(a, b, dims=((1,), (0,))):
    return lax.dot_general(a, b, (dims, ((), ())), preferred_element_type=jnp.float32)


def pack_kernel(devices, block, dest_ref, pep_ref, send_ref, pos_ref, meta_ref):
    step = pl.program_id(0)
    rows = pep_ref.shape[0]
    width = pep_ref.shape[1]

    @pl.when(step == 0)
    def _():
        dest = dest_ref[...]
        owner = lax.shift_right_logical(dest, log2(rows))
        filled = dest - owner * rows + 1
        member = iota((devices, rows), 0) == owner
        before = onehot(iota((rows, rows), 0) < iota((rows, rows), 1))
        seen = matmul(onehot(member), before)
        rank = jnp.sum(jnp.where(member, seen, 0.0), axis=0, keepdims=True).astype(jnp.int32)
        position = owner * block + rank
        for c in range(rows // CHUNK):
            pos_ref[c : c + 1, :] = position[:, c * CHUNK : (c + 1) * CHUNK]
        high = lax.shift_right_logical(filled, log2(BASE))
        low = filled - high * BASE
        lane = iota((2 * CHUNK, rows), 0)
        part = jnp.where(lane < CHUNK, high.astype(jnp.float32), low.astype(jnp.float32))
        spread = jnp.where((lane & (block - 1)) == rank, part, 0.0).astype(jnp.bfloat16)
        meta_ref[...] = matmul(onehot(member), spread, ((1,), (1,))).astype(jnp.bfloat16)

    base = step * CHUNK
    position = jnp.concatenate([pos_ref[c : c + 1, :] for c in range(rows // CHUNK)], axis=1)
    pick = onehot(iota((CHUNK, rows), 0) + base == position)
    place = onehot(
        iota((CHUNK, devices), 0) + base == iota((CHUNK, devices), 1) * block + (block - 1)
    )
    sent = matmul(pick, pep_ref[...])
    extra = matmul(place, meta_ref[...])
    send_ref[...] = (sent + extra).astype(jnp.bfloat16)


def pack(destination, peptides, devices, block):
    rows, width = peptides.shape
    slots = devices * block
    assert width == 2 * CHUNK and CHUNK % block == 0 and slots % CHUNK == 0
    return pl.pallas_call(
        functools.partial(pack_kernel, devices, block),
        grid=(slots // CHUNK,),
        in_specs=[
            pl.BlockSpec((1, rows), lambda c: (0, 0)),
            pl.BlockSpec((rows, width), lambda c: (0, 0)),
        ],
        out_specs=[
            pl.BlockSpec((CHUNK, width), lambda c: (c, 0)),
            pl.BlockSpec((rows // CHUNK, CHUNK), lambda c: (0, 0)),
        ],
        out_shape=[
            jax.ShapeDtypeStruct((slots, width), jnp.bfloat16),
            jax.ShapeDtypeStruct((rows // CHUNK, CHUNK), jnp.int32),
        ],
        scratch_shapes=[pltpu.VMEM((devices, width), jnp.bfloat16)],
        name="pack",
    )(destination.reshape(1, rows), peptides)


def unpack_kernel(block, got_ref, table_ref, slot_ref, pick_ref):
    step = pl.program_id(0)
    chunks = got_ref.shape[0] // CHUNK

    @pl.when(step == 0)
    def _():
        lane = iota((CHUNK, CHUNK), 1)
        tail = iota((CHUNK, CHUNK), 0) == lane - (lane & (block - 1)) + (block - 1)
        for q in range(chunks):
            part = got_ref[q * CHUNK : (q + 1) * CHUNK, :].astype(jnp.float32)
            high = jnp.sum(jnp.where(tail, part[:, :CHUNK], 0.0), axis=0, keepdims=True)
            low = jnp.sum(jnp.where(tail, part[:, CHUNK:], 0.0), axis=0, keepdims=True)
            slot_ref[q : q + 1, :] = (high * BASE + low).astype(jnp.int32) - 1

    row = iota((CHUNK, CHUNK), 0) + step * CHUNK
    for q in range(chunks):
        pick_ref[:, q * CHUNK : (q + 1) * CHUNK] = onehot(row == slot_ref[q : q + 1, :])
    table_ref[...] = matmul(pick_ref[...], got_ref[...]).astype(jnp.bfloat16)


def unpack(got, rows, block):
    slots, width = got.shape
    return pl.pallas_call(
        functools.partial(unpack_kernel, block),
        grid=(rows // CHUNK,),
        in_specs=[pl.BlockSpec((slots, width), lambda c: (0, 0))],
        out_specs=[
            pl.BlockSpec((CHUNK, width), lambda c: (c, 0)),
            pl.BlockSpec((slots // CHUNK, CHUNK), lambda c: (0, 0)),
        ],
        out_shape=[
            jax.ShapeDtypeStruct((rows, width), jnp.bfloat16),
            jax.ShapeDtypeStruct((slots // CHUNK, CHUNK), jnp.int32),
        ],
        scratch_shapes=[pltpu.VMEM((CHUNK, slots), jnp.bfloat16)],
        name="unpack",
    )(got)


def main_kernel(
    band_ref,
    factor_ref,
    before_ref,
    own_ref,
    after_ref,
    spec_ref,
    pos_ref,
    spec_grad_ref,
    left_ref,
    mine_ref,
    right_ref,
    ext_ref,
    grad_ref,
    sems,
):
    k = pl.program_id(0)
    edge = EDGE * TILE_ROWS
    mine = TILE_DEV * TILE_ROWS
    scaling = factor_ref[0]
    offset = factor_ref[1]

    @pl.when(k == 0)
    def _():
        copies = [
            pltpu.make_async_copy(before_ref, ext_ref.at[pl.ds(0, edge)], sems.at[0]),
            pltpu.make_async_copy(own_ref, ext_ref.at[pl.ds(edge, mine)], sems.at[1]),
            pltpu.make_async_copy(after_ref, ext_ref.at[pl.ds(edge + mine, edge)], sems.at[2]),
        ]
        for copy in copies:
            copy.start()
        grad_ref[...] = jnp.zeros_like(grad_ref)
        for copy in copies:
            copy.wait()

    spec = spec_ref[...]
    wanted = pos_ref[0]
    row = iota((TILE_ROWS, TILE_ROWS), 0)
    total = jnp.zeros(spec.shape, jnp.float32)
    for j in range(NB):
        start = pl.multiple_of(band_ref[k * NB + j] * TILE_ROWS, TILE_ROWS)
        tile = ext_ref[pl.ds(start, TILE_ROWS), :]
        logits = scaling * matmul(tile, spec, ((1,), (1,))) + offset
        labels = jnp.where(row + j * TILE_ROWS == wanted, 1.0, 0.0)
        weights = (jax.nn.sigmoid(logits) - labels).astype(jnp.bfloat16)
        grad_ref[pl.ds(start, TILE_ROWS), :] += matmul(weights, spec)
        total += matmul(weights, tile, ((0,), (0,)))
    spec_grad_ref[...] = (scaling * total).astype(jnp.bfloat16)

    @pl.when(k == SB - 1)
    def _():
        left_ref[...] = (scaling * grad_ref[:edge, :]).astype(jnp.bfloat16)
        mine_ref[...] = scaling * grad_ref[edge : edge + mine, :]
        right_ref[...] = (scaling * grad_ref[edge + mine :, :]).astype(jnp.bfloat16)


def gradients(band, factors, before, own, after, spectra, positive):
    width = spectra.shape[1]
    edge = EDGE * TILE_ROWS
    mine = TILE_DEV * TILE_ROWS
    anywhere = pl.BlockSpec(memory_space=pl.ANY)
    whole = lambda r: pl.BlockSpec((r, width), lambda k, *_: (0, 0))
    return pl.pallas_call(
        main_kernel,
        grid_spec=pltpu.PrefetchScalarGridSpec(
            num_scalar_prefetch=2,
            grid=(SB,),
            in_specs=[
                anywhere,
                anywhere,
                anywhere,
                pl.BlockSpec((TILE_ROWS, width), lambda k, *_: (k, 0)),
                pl.BlockSpec((1, 1, TILE_ROWS), lambda k, *_: (k, 0, 0)),
            ],
            out_specs=[
                pl.BlockSpec((TILE_ROWS, width), lambda k, *_: (k, 0)),
                whole(edge),
                whole(mine),
                whole(edge),
            ],
            scratch_shapes=[
                pltpu.VMEM((2 * edge + mine, width), jnp.bfloat16),
                pltpu.VMEM((2 * edge + mine, width), jnp.float32),
                pltpu.SemaphoreType.DMA((3,)),
            ],
        ),
        out_shape=[
            jax.ShapeDtypeStruct((SB * TILE_ROWS, width), jnp.bfloat16),
            jax.ShapeDtypeStruct((edge, width), jnp.bfloat16),
            jax.ShapeDtypeStruct((mine, width), jnp.float32),
            jax.ShapeDtypeStruct((edge, width), jnp.bfloat16),
        ],
        name="gradients",
    )(band, factors, before, own, after, spectra, positive)


def columns_of(row):
    tall = jnp.broadcast_to(row.astype(jnp.float32), (128, row.shape[1]))
    return jnp.transpose(tall).astype(jnp.int32)


def back_kernel(slot_ref, mine_ref, left_ref, right_ref, back_ref, grad_ref, pick_ref):
    step = pl.program_id(0)
    rows = mine_ref.shape[0]
    edge = left_ref.shape[0]

    @pl.when(step == 0)
    def _():
        lower = mine_ref[:edge, :] + left_ref[...].astype(jnp.float32)
        grad_ref[:edge, :] = lower.astype(jnp.bfloat16)
        upper = mine_ref[rows - edge :, :] + right_ref[...].astype(jnp.float32)
        grad_ref[rows - edge :, :] = upper.astype(jnp.bfloat16)

    slot = columns_of(slot_ref[pl.ds(step, 1), :])
    lane = iota(slot.shape, 1)
    for m in range(rows // 128):
        pick_ref[:, m * 128 : (m + 1) * 128] = onehot(lane + m * 128 == slot)
    back_ref[...] = matmul(pick_ref[...], grad_ref[...]).astype(jnp.bfloat16)


def send_back(slot, mine, from_left, from_right):
    rows, width = mine.shape
    edge = from_left.shape[0]
    assert rows == 2 * edge
    chunks = slot.shape[0]
    return pl.pallas_call(
        back_kernel,
        grid=(chunks,),
        in_specs=[
            pl.BlockSpec((chunks, CHUNK), lambda c: (0, 0)),
            pl.BlockSpec((rows, width), lambda c: (0, 0)),
            pl.BlockSpec((edge, width), lambda c: (0, 0)),
            pl.BlockSpec((edge, width), lambda c: (0, 0)),
        ],
        out_specs=pl.BlockSpec((CHUNK, width), lambda c: (c, 0)),
        out_shape=jax.ShapeDtypeStruct((chunks * CHUNK, width), jnp.bfloat16),
        scratch_shapes=[
            pltpu.VMEM((rows, width), jnp.bfloat16),
            pltpu.VMEM((CHUNK, rows), jnp.bfloat16),
        ],
        name="send_back",
    )(slot, mine, from_left, from_right)


def home_kernel(pos_ref, got_ref, out_ref, pick_ref):
    step = pl.program_id(0)
    position = columns_of(pos_ref[pl.ds(step, 1), :])
    lane = iota(position.shape, 1)
    for m in range(got_ref.shape[0] // 128):
        pick_ref[:, m * 128 : (m + 1) * 128] = onehot(lane + m * 128 == position)
    out_ref[...] = matmul(pick_ref[...], got_ref[...]).astype(jnp.bfloat16)


def home(position, returned):
    slots, width = returned.shape
    chunks = position.shape[0]
    return pl.pallas_call(
        home_kernel,
        grid=(chunks,),
        in_specs=[
            pl.BlockSpec((chunks, CHUNK), lambda c: (0, 0)),
            pl.BlockSpec((slots, width), lambda c: (0, 0)),
        ],
        out_specs=pl.BlockSpec((CHUNK, width), lambda c: (c, 0)),
        out_shape=jax.ShapeDtypeStruct((chunks * CHUNK, width), jnp.bfloat16),
        scratch_shapes=[pltpu.VMEM((CHUNK, slots), jnp.bfloat16)],
        name="home",
    )(position, returned)


def shifted(value, steps):
    count = lax.axis_size("mass") * lax.axis_size("prot")
    first, last = (max(0, -steps), min(count, count - steps))
    return lax.ppermute(value, AXES, [(source, source + steps) for source in range(first, last)])


def body(spectra, peptides, destination, band, positive, logit_scale, logit_bias):
    devices = lax.axis_size("mass") * lax.axis_size("prot")
    rows, width = peptides.shape
    edge = EDGE * TILE_ROWS
    block = 2 * (rows // devices)
    factors = jnp.concatenate([logit_scale / math.sqrt(width), logit_bias])

    send, position = pack(destination, peptides, devices, block)
    got = lax.all_to_all(send, AXES, 0, 0, tiled=True)
    table, slot = unpack(got, rows, block)
    before = shifted(table[rows - edge :], 1)
    after = shifted(table[:edge], -1)
    spec_grad, to_left, mine, to_right = gradients(
        band.reshape(-1), factors, before, table, after, spectra,
        positive.reshape(SB, 1, TILE_ROWS),
    )
    from_right = shifted(to_left, -1)
    from_left = shifted(to_right, 1)
    back = send_back(slot, mine, from_left, from_right)
    returned = lax.all_to_all(back, AXES, 0, 0, tiled=True)
    return (spec_grad, home(position, returned))


def solution(mesh):
    in_specs = (
        P(AXES, None),
        P(AXES, None),
        P(AXES),
        P(AXES, None),
        P(AXES),
        P(),
        P(),
    )
    out_specs = (P(AXES, None), P(AXES, None))
    return jax.shard_map(body, mesh=mesh, in_specs=in_specs, out_specs=out_specs, check_vma=False)
```

```python
import functools
import math

import jax
import jax.numpy as jnp
from jax import lax
from jax.experimental import pallas as pl
from jax.experimental.pallas import tpu as pltpu
from jax.sharding import PartitionSpec as P


TILE_ROWS = 256
EDGE = 2
NB = 6
TILE_DEV = 4
SB = 4
CHUNK = 256
AXES = ("mass", "prot")
BASE = 256
GROUP = 2
WIDE = GROUP * CHUNK
VMEM_LIMIT = 24 * 1024 * 1024
PARAMS = pltpu.CompilerParams(vmem_limit_bytes=VMEM_LIMIT)
IN_VMEM = pl.BlockSpec(memory_space=pltpu.VMEM)
IN_SMEM = pl.BlockSpec(memory_space=pltpu.SMEM)
ANYWHERE = pl.BlockSpec(memory_space=pl.ANY)
IN_HBM = pl.BlockSpec(memory_space=pltpu.HBM)


def log2(value):
    bits = value.bit_length() - 1
    assert value == 1 << bits
    return bits


def iota(shape, dim):
    return lax.broadcasted_iota(jnp.int32, shape, dim)


def onehot(mask):
    return jnp.where(mask, 1.0, 0.0).astype(jnp.bfloat16)


def matmul(a, b, dims=((1,), (0,))):
    return lax.dot_general(a, b, (dims, ((), ())), preferred_element_type=jnp.float32)


def chunk_copy(source, target, sems, c):
    part = pl.ds(pl.multiple_of(c * WIDE, WIDE), WIDE)
    return pltpu.make_async_copy(source.at[part], target.at[part], sems.at[c])


def in_hbm(value):
    return pltpu.with_memory_space_constraint(value, pltpu.HBM)


def pack_kernel(
    devices,
    block,
    dest_any,
    pep_any,
    want_any,
    band_any,
    send_ref,
    pos_ref,
    info_ref,
    dest_ref,
    pep_ref,
    want_ref,
    band_ref,
    meta_ref,
    rows_ref,
    load_sems,
    sems,
):
    rows = pep_ref.shape[0]
    pairs = [(dest_any, dest_ref), (want_any, want_ref), (band_any, band_ref), (pep_any, pep_ref)]
    loads = [pltpu.make_async_copy(*pair, load_sems.at[n]) for n, pair in enumerate(pairs)]
    for load in loads:
        load.start()
    for load in loads[:3]:
        load.wait()
    info_ref[...] = jnp.zeros_like(info_ref)
    for k in range(SB):
        info_ref[k : k + 1, :] = want_ref[k]
    info_ref[SB:, :NB] = band_ref[...] + 1

    dest = dest_ref[...]
    owner = lax.shift_right_logical(dest, log2(rows))
    filled = dest - owner * rows + 1
    member = iota((devices, rows), 0) == owner
    before = onehot(iota((rows, rows), 0) < iota((rows, rows), 1))
    seen = matmul(onehot(member), before)
    rank = jnp.sum(jnp.where(member, seen, 0.0), axis=0, keepdims=True).astype(jnp.int32)
    position = owner * block + rank
    for c in range(rows // CHUNK):
        pos_ref[c : c + 1, :] = position[:, c * CHUNK : (c + 1) * CHUNK]
    high = lax.shift_right_logical(filled, log2(BASE))
    low = filled - high * BASE
    lane = iota((2 * CHUNK, rows), 0)
    part = jnp.where(lane < CHUNK, high.astype(jnp.float32), low.astype(jnp.float32))
    spread = jnp.where((lane & (block - 1)) == rank, part, 0.0).astype(jnp.bfloat16)
    meta_ref[...] = matmul(onehot(member), spread, ((1,), (1,))).astype(jnp.bfloat16)

    loads[3].wait()

    def chunk(c, carry):
        base = c * WIDE
        place = jnp.concatenate([pos_ref[q : q + 1, :] for q in range(rows // CHUNK)], axis=1)
        pick = onehot(iota((WIDE, rows), 0) + base == place)
        tail = onehot(
            iota((WIDE, devices), 0) + base == iota((WIDE, devices), 1) * block + (block - 1)
        )
        sent = matmul(pick, pep_ref[...]) + matmul(tail, meta_ref[...])
        rows_ref[pl.ds(pl.multiple_of(base, WIDE), WIDE), :] = sent.astype(jnp.bfloat16)
        chunk_copy(rows_ref, send_ref, sems, c).start()
        return carry

    lax.fori_loop(0, send_ref.shape[0] // WIDE, chunk, 0)
    for c in range(send_ref.shape[0] // WIDE):
        chunk_copy(rows_ref, send_ref, sems, c).wait()


def pack(destination, peptides, positive, band, devices, block):
    rows, width = peptides.shape
    slots = devices * block
    operands = (
        destination.reshape(1, rows), peptides, positive.reshape(SB, 1, TILE_ROWS), band
    )
    assert width == 2 * CHUNK and CHUNK % block == 0 and slots % WIDE == 0
    return pl.pallas_call(
        functools.partial(pack_kernel, devices, block),
        in_specs=[IN_HBM] * 4,
        out_specs=[IN_HBM, IN_VMEM, IN_VMEM],
        out_shape=[
            pltpu.HBM((slots, width), jnp.bfloat16),
            jax.ShapeDtypeStruct((rows // CHUNK, CHUNK), jnp.int32),
            jax.ShapeDtypeStruct((2 * SB, TILE_ROWS), jnp.int32),
        ],
        scratch_shapes=[
            pltpu.VMEM((1, rows), jnp.int32),
            pltpu.VMEM((rows, width), jnp.bfloat16),
            pltpu.VMEM((SB, 1, TILE_ROWS), jnp.int32),
            pltpu.VMEM((SB, NB), jnp.int32),
            pltpu.VMEM((devices, width), jnp.bfloat16),
            pltpu.VMEM((slots, width), jnp.bfloat16),
            pltpu.SemaphoreType.DMA((4,)),
            pltpu.SemaphoreType.DMA((slots // WIDE,)),
        ],
        compiler_params=PARAMS,
        name="pack",
    )(*map(in_hbm, operands))


def columns_of(row):
    tall = jnp.broadcast_to(row.astype(jnp.float32), (128, row.shape[1]))
    return jnp.transpose(tall).astype(jnp.int32)


def weights_of(logits, half_scale, half_offset, wanted, shift):
    hit = iota(logits.shape, 0) + shift == wanted
    base = jnp.where(hit, -0.5, 0.5)
    return (0.5 * jnp.tanh(logits * half_scale + half_offset) + base).astype(jnp.bfloat16)


def unpack_kernel(
    block,
    got_ref,
    spec_prev,
    spec_own,
    spec_next,
    table_ref,
    slot_ref,
    spec_ref,
    low_ref,
    high_ref,
    pick_ref,
    spec_sems,
    sems,
):
    chunks = got_ref.shape[0] // CHUNK
    dev_rows = SB * TILE_ROWS
    loads = [
        pltpu.make_async_copy(spec, spec_ref.at[pl.ds(n * dev_rows, dev_rows)], spec_sems.at[n])
        for n, spec in enumerate((spec_prev, spec_own, spec_next))
    ]
    for load in loads:
        load.start()

    lane = iota((CHUNK, CHUNK), 1)
    tail = iota((CHUNK, CHUNK), 0) == lane - (lane & (block - 1)) + (block - 1)
    for q in range(chunks):
        part = got_ref[q * CHUNK : (q + 1) * CHUNK, :].astype(jnp.float32)
        high = jnp.sum(jnp.where(tail, part[:, :CHUNK], 0.0), axis=0, keepdims=True)
        low = jnp.sum(jnp.where(tail, part[:, CHUNK:], 0.0), axis=0, keepdims=True)
        slot_ref[q : q + 1, :] = (high * BASE + low).astype(jnp.int32) - 1

    stores = []
    for half, edge_ref in enumerate((low_ref, high_ref)):

        edge = EDGE * TILE_ROWS
        row = iota((edge, CHUNK), 0) + half * edge
        for q in range(chunks):
            pick_ref[:, q * CHUNK : (q + 1) * CHUNK] = onehot(row == slot_ref[q : q + 1, :])
        half_table = matmul(pick_ref[...], got_ref[...]).astype(jnp.bfloat16)
        table_ref[half * edge : (half + 1) * edge, :] = half_table
        store = pltpu.make_async_copy(
            table_ref.at[pl.ds(half * edge, edge)], edge_ref, sems.at[half]
        )
        store.start()
        stores.append(store)
    for copy in stores + loads:
        copy.wait()


def unpack(got, spectra, block):
    slots, width = got.shape
    rows = TILE_DEV * TILE_ROWS
    chunks = slots // CHUNK
    assert TILE_DEV == 2 * EDGE and CHUNK == TILE_ROWS
    half = pltpu.HBM((rows // 2, width), jnp.bfloat16)
    return pl.pallas_call(
        functools.partial(unpack_kernel, block),
        in_specs=[IN_VMEM] + [ANYWHERE] * 3,
        out_specs=[IN_VMEM] * 3 + [IN_HBM] * 2,
        out_shape=[
            jax.ShapeDtypeStruct((rows, width), jnp.bfloat16),
            jax.ShapeDtypeStruct((chunks, CHUNK), jnp.int32),
            jax.ShapeDtypeStruct((3 * SB * TILE_ROWS, width), jnp.bfloat16),
            half,
            half,
        ],
        scratch_shapes=[
            pltpu.VMEM((EDGE * TILE_ROWS, slots), jnp.bfloat16),
            pltpu.SemaphoreType.DMA((3,)),
            pltpu.SemaphoreType.DMA((2,)),
        ],
        compiler_params=PARAMS,
        name="unpack",
    )(got, *map(in_hbm, spectra))


def tiles_kernel(
    scale_ref,
    bias_ref,
    table_ref,
    slot_ref,
    spec_ref,
    info_prev,
    info_own,
    info_next,
    band_prev,
    band_own,
    band_next,
    back_ref,
    mask_ref,
    weight_ref,
    grad_ref,
    rows_ref,
    sems,
):
    chunks = slot_ref.shape[0]
    rows = grad_ref.shape[0]
    dev_rows = SB * TILE_ROWS
    scaling = scale_ref[0] * (1.0 / math.sqrt(table_ref.shape[1]))
    infos = (info_prev, info_own, info_next)
    bands = (band_prev, band_own, band_next)

    edge = EDGE * TILE_ROWS
    for upper in range(TILE_DEV // EDGE):
        pair = table_ref[upper * edge : (upper + 1) * edge, :]
        for source in (upper, upper + 1):
            for k in range(SB):
                first = (source * SB + k) * TILE_ROWS
                column = first - upper * dev_rows
                logits = matmul(pair, spec_ref[first : first + TILE_ROWS, :], ((1,), (1,)))
                for e in range(EDGE):
                    tag = upper * EDGE + e + (EDGE + TILE_DEV * (1 - source) + 1)
                    place = jnp.int32(-1)
                    for j in range(NB):
                        place = jnp.where(bands[source][SB + k, j] == tag, j, place)
                    active = place >= 0
                    span = slice(e * TILE_ROWS, (e + 1) * TILE_ROWS)
                    weight_ref[span, column : column + TILE_ROWS] = weights_of(
                        logits[span, :],
                        jnp.where(active, 0.5 * scaling, 0.0),
                        jnp.where(active, 0.5 * bias_ref[0], -1e30),
                        infos[source][k : k + 1, :],
                        jnp.where(active, place, 2 * NB) * TILE_ROWS,
                    )
        total = matmul(weight_ref[...], spec_ref[upper * dev_rows : (upper + 2) * dev_rows, :])
        grad_ref[upper * edge : (upper + 1) * edge, :] = (scaling * total).astype(jnp.bfloat16)

    def back_step(q, carry):
        for g in range(GROUP):
            slot = columns_of(slot_ref[pl.ds(q * GROUP + g, 1), :])
            lane = iota(slot.shape, 1)
            for m in range(rows // 128):
                mask_ref[g * CHUNK : (g + 1) * CHUNK, m * 128 : (m + 1) * 128] = onehot(
                    lane + m * 128 == slot
                )
        start = pl.multiple_of(q * WIDE, WIDE)
        rows_ref[pl.ds(start, WIDE), :] = matmul(mask_ref[...], grad_ref[...]).astype(jnp.bfloat16)
        chunk_copy(rows_ref, back_ref, sems, q).start()
        return carry

    lax.fori_loop(0, chunks // GROUP, back_step, 0)
    for q in range(chunks // GROUP):
        chunk_copy(rows_ref, back_ref, sems, q).wait()


def tiles(scale, bias, table, slot, spectra, infos):
    rows, width = table.shape
    chunks = slot.shape[0]
    slots = chunks * CHUNK
    return pl.pallas_call(
        tiles_kernel,
        in_specs=[IN_SMEM] * 2 + [IN_VMEM] * 6 + [IN_SMEM] * 3,
        out_specs=IN_HBM,
        out_shape=pltpu.HBM((slots, width), jnp.bfloat16),
        scratch_shapes=[
            pltpu.VMEM((WIDE, rows), jnp.bfloat16),
            pltpu.VMEM((EDGE * TILE_ROWS, 2 * SB * TILE_ROWS), jnp.bfloat16),
            pltpu.VMEM((rows, width), jnp.bfloat16),
            pltpu.VMEM((slots, width), jnp.bfloat16),
            pltpu.SemaphoreType.DMA((chunks,)),
        ],
        compiler_params=PARAMS,
        name="tiles",
    )(scale, bias, table, slot, spectra, *infos, *infos)


def spectra_kernel(
    scale_ref, bias_ref, band_ref, before_ref, own_ref, after_ref, spec_ref, info_ref,
    out_ref, ext_ref, sems,
):
    k = pl.program_id(0)
    edge = EDGE * TILE_ROWS
    scaling = scale_ref[0] * (1.0 / math.sqrt(out_ref.shape[1]))

    @pl.when(k == 0)
    def _():
        mine = TILE_DEV * TILE_ROWS
        copies = [
            pltpu.make_async_copy(before_ref, ext_ref.at[pl.ds(0, edge)], sems.at[0]),
            pltpu.make_async_copy(own_ref, ext_ref.at[pl.ds(edge, mine)], sems.at[1]),
            pltpu.make_async_copy(after_ref, ext_ref.at[pl.ds(edge + mine, edge)], sems.at[2]),
        ]
        for copy in copies:
            copy.start()
        for copy in copies:
            copy.wait()

    total = jnp.zeros(out_ref.shape, jnp.float32)
    for j in range(NB):
        start = pl.multiple_of((band_ref[SB + k, j] - 1) * TILE_ROWS, TILE_ROWS)
        tile = ext_ref[pl.ds(start, TILE_ROWS), :]
        weights = weights_of(
            matmul(tile, spec_ref[...], ((1,), (1,))),
            0.5 * scaling,
            0.5 * bias_ref[0],
            info_ref[pl.ds(k, 1), :],
            j * TILE_ROWS,
        )
        total += matmul(weights, tile, ((0,), (0,)))
    out_ref[...] = (scaling * total).astype(jnp.bfloat16)


def spectra_gradient(scale, bias, info, before, table, after, spectra):
    width = spectra.shape[1]
    edge = EDGE * TILE_ROWS
    return pl.pallas_call(
        spectra_kernel,
        grid=(SB,),
        in_specs=[
            IN_SMEM,
            IN_SMEM,
            IN_SMEM,
            ANYWHERE,
            ANYWHERE,
            ANYWHERE,
            pl.BlockSpec((TILE_ROWS, width), lambda k: (k, 0)),
            pl.BlockSpec((2 * SB, TILE_ROWS), lambda k: (0, 0)),
        ],
        out_specs=pl.BlockSpec((TILE_ROWS, width), lambda k: (k, 0)),
        scratch_shapes=[
            pltpu.VMEM((4 * edge, width), jnp.bfloat16),
            pltpu.SemaphoreType.DMA((3,)),
        ],
        compiler_params=PARAMS,
        out_shape=jax.ShapeDtypeStruct((SB * TILE_ROWS, width), jnp.bfloat16),
        name="spectra_gradient",
    )(scale, bias, info, before, table, after, spectra, info)


def home_kernel(pos_ref, got_ref, out_ref, pick_ref, grad_ref, sems):
    chunks = pos_ref.shape[0]

    def chunk(c, carry):
        for g in range(GROUP):
            position = columns_of(pos_ref[pl.ds(c * GROUP + g, 1), :])
            lane = iota(position.shape, 1)
            for m in range(got_ref.shape[0] // 128):
                pick_ref[g * CHUNK : (g + 1) * CHUNK, m * 128 : (m + 1) * 128] = onehot(
                    lane + m * 128 == position
                )
        grad = matmul(pick_ref[...], got_ref[...]).astype(jnp.bfloat16)
        grad_ref[pl.ds(pl.multiple_of(c * WIDE, WIDE), WIDE), :] = grad
        chunk_copy(grad_ref, out_ref, sems, c).start()
        return carry

    lax.fori_loop(0, chunks // GROUP, chunk, 0)
    for c in range(chunks // GROUP):
        chunk_copy(grad_ref, out_ref, sems, c).wait()


def home(position, returned):
    slots, width = returned.shape
    chunks = position.shape[0]
    rows = chunks * CHUNK
    return pl.pallas_call(
        home_kernel,
        in_specs=[IN_VMEM] * 2,
        out_specs=IN_HBM,
        out_shape=jax.ShapeDtypeStruct((rows, width), jnp.bfloat16),
        scratch_shapes=[
            pltpu.VMEM((WIDE, slots), jnp.bfloat16),
            pltpu.VMEM((rows, width), jnp.bfloat16),
            pltpu.SemaphoreType.DMA((chunks,)),
        ],
        compiler_params=PARAMS,
        name="home",
    )(position, returned)


def shifted(value, steps):
    count = lax.axis_size("mass") * lax.axis_size("prot")
    first, last = (max(0, -steps), min(count, count - steps))
    return lax.ppermute(value, AXES, [(source, source + steps) for source in range(first, last)])


def program(spectra, peptides, destination, band, positive, logit_scale, logit_bias):
    devices = lax.axis_size("mass") * lax.axis_size("prot")
    rows = peptides.shape[0]
    block = 2 * (rows // devices)

    spec_prev = shifted(spectra, 1)
    spec_next = shifted(spectra, -1)
    send, position, info = pack(destination, peptides, positive, band, devices, block)
    info_prev = shifted(info, 1)
    info_next = shifted(info, -1)
    got = lax.all_to_all(send, AXES, 0, 0, tiled=True)
    table, slot, specs, low, high = unpack(got, (spec_prev, spectra, spec_next), block)
    after = shifted(low, -1)
    before = shifted(high, 1)
    back = tiles(logit_scale, logit_bias, table, slot, specs, (info_prev, info, info_next))
    returned = lax.all_to_all(back, AXES, 0, 0, tiled=True)
    spec_grad = spectra_gradient(logit_scale, logit_bias, info, before, table, after, spectra)
    return (spec_grad, home(position, returned))


def solution(mesh):
    in_specs = (
        P(AXES, None),
        P(AXES, None),
        P(AXES),
        P(AXES, None),
        P(AXES),
        P(),
        P(),
    )
    out_specs = (P(AXES, None), P(AXES, None))
    return jax.shard_map(program, mesh=mesh, in_specs=in_specs, out_specs=out_specs, check_vma=False)
```

```python
import functools
import math

import jax
import jax.numpy as jnp
from jax import lax
from jax.experimental import pallas as pl
from jax.experimental.pallas import tpu as pltpu
from jax.sharding import PartitionSpec as P


TILE_ROWS = 256
EDGE = 2
NB = 6
TILE_DEV = 4
SB = 4
CHUNK = 256
AXES = ("mass", "prot")
BASE = 256
GROUP = 2
WIDE = GROUP * CHUNK
LANES = 128
VMEM_LIMIT = 24 * 1024 * 1024
PARAMS = pltpu.CompilerParams(vmem_limit_bytes=VMEM_LIMIT)
IN_VMEM = pl.BlockSpec(memory_space=pltpu.VMEM)
IN_SMEM = pl.BlockSpec(memory_space=pltpu.SMEM)
ANYWHERE = pl.BlockSpec(memory_space=pl.ANY)
IN_HBM = pl.BlockSpec(memory_space=pltpu.HBM)


def log2(value):
    bits = value.bit_length() - 1
    assert value == 1 << bits
    return bits


def iota(shape, dim):
    return lax.broadcasted_iota(jnp.int32, shape, dim)


def onehot(mask):
    return jnp.where(mask, 1.0, 0.0).astype(jnp.bfloat16)


def matmul(a, b, dims=((1,), (0,))):
    return lax.dot_general(a, b, (dims, ((), ())), preferred_element_type=jnp.float32)


def chunk_copy(source, target, sems, c):
    part = pl.ds(pl.multiple_of(c * WIDE, WIDE), WIDE)
    return pltpu.make_async_copy(source.at[part], target.at[part], sems.at[c])


def in_hbm(value):
    return pltpu.with_memory_space_constraint(value, pltpu.HBM)


def pack_kernel(
    devices,
    block,
    dest_any,
    pep_any,
    want_any,
    band_any,
    send_ref,
    pos_ref,
    info_ref,
    dest_ref,
    pep_ref,
    want_ref,
    band_ref,
    meta_ref,
    lower_ref,
    upper_ref,
    rows_ref,
    load_sems,
    sems,
):
    rows = pep_ref.shape[0]
    pairs = [(dest_any, dest_ref), (want_any, want_ref), (band_any, band_ref), (pep_any, pep_ref)]
    loads = [pltpu.make_async_copy(*pair, load_sems.at[n]) for n, pair in enumerate(pairs)]
    for load in loads:
        load.start()
    for load in loads[:3]:
        load.wait()
    info_ref[...] = jnp.zeros_like(info_ref)
    for k in range(SB):
        info_ref[k : k + 1, :] = want_ref[k]
    info_ref[SB:, :NB] = band_ref[...] + 1

    dest = dest_ref[...]
    owner = lax.shift_right_logical(dest, log2(rows))
    filled = dest - owner * rows + 1
    member = iota((devices, rows), 0) == owner
    groups = [
        jnp.where(member[:, g : g + LANES], 1.0, 0.0) for g in range(0, rows, LANES)
    ]
    earlier = onehot(iota((LANES, LANES), 0) < iota((LANES, LANES), 1))
    seen = []
    count = jnp.zeros((devices, 1), jnp.float32)
    for group in groups:
        inside = matmul(group.astype(jnp.bfloat16), earlier) + count
        seen.append(jnp.sum(group * inside, axis=0, keepdims=True))
        count = count + jnp.sum(group, axis=1, keepdims=True)
    rank = jnp.concatenate(seen, axis=1).astype(jnp.int32)
    position = owner * block + rank
    for c in range(rows // CHUNK):
        pos_ref[c : c + 1, :] = position[:, c * CHUNK : (c + 1) * CHUNK]
    high = lax.shift_right_logical(filled, log2(BASE))
    low = filled - high * BASE
    lane = iota((2 * CHUNK, rows), 0)
    part = jnp.where(lane < CHUNK, high.astype(jnp.float32), low.astype(jnp.float32))
    spread = jnp.where((lane & (block - 1)) == rank, part, 0.0).astype(jnp.bfloat16)
    meta_ref[...] = matmul(onehot(member), spread, ((1,), (1,))).astype(jnp.bfloat16)
    lower_ref[...] = onehot(iota((CHUNK, rows), 0) == (position & (CHUNK - 1)))
    upper_ref[...] = lax.shift_right_logical(position, log2(CHUNK))
    loads[3].wait()

    def chunk(c, carry):
        base = c * WIDE
        pick = jnp.concatenate(
            [lower_ref[...] * onehot(upper_ref[...] == c * GROUP + g) for g in range(GROUP)], axis=0
        )
        tail = onehot(
            iota((WIDE, devices), 0) + base == iota((WIDE, devices), 1) * block + (block - 1)
        )
        sent = matmul(pick, pep_ref[...]) + matmul(tail, meta_ref[...])
        rows_ref[pl.ds(pl.multiple_of(base, WIDE), WIDE), :] = sent.astype(jnp.bfloat16)
        chunk_copy(rows_ref, send_ref, sems, c).start()
        return carry

    lax.fori_loop(0, send_ref.shape[0] // WIDE, chunk, 0)
    for c in range(send_ref.shape[0] // WIDE):
        chunk_copy(rows_ref, send_ref, sems, c).wait()


def pack(destination, peptides, positive, band, devices, block):
    rows, width = peptides.shape
    slots = devices * block
    operands = (
        destination.reshape(1, rows), peptides, positive.reshape(SB, 1, TILE_ROWS), band
    )
    assert width == 2 * CHUNK and CHUNK % block == 0 and slots % WIDE == 0
    return pl.pallas_call(
        functools.partial(pack_kernel, devices, block),
        in_specs=[IN_HBM] * 4,
        out_specs=[IN_HBM, IN_VMEM, IN_VMEM],
        out_shape=[
            pltpu.HBM((slots, width), jnp.bfloat16),
            jax.ShapeDtypeStruct((rows // CHUNK, CHUNK), jnp.int32),
            jax.ShapeDtypeStruct((2 * SB, TILE_ROWS), jnp.int32),
        ],
        scratch_shapes=[
            pltpu.VMEM((1, rows), jnp.int32),
            pltpu.VMEM((rows, width), jnp.bfloat16),
            pltpu.VMEM((SB, 1, TILE_ROWS), jnp.int32),
            pltpu.VMEM((SB, NB), jnp.int32),
            pltpu.VMEM((devices, width), jnp.bfloat16),
            pltpu.VMEM((CHUNK, rows), jnp.bfloat16),
            pltpu.VMEM((1, rows), jnp.int32),
            pltpu.VMEM((slots, width), jnp.bfloat16),
            pltpu.SemaphoreType.DMA((4,)),
            pltpu.SemaphoreType.DMA((slots // WIDE,)),
        ],
        compiler_params=PARAMS,
        name="pack",
    )(*map(in_hbm, operands))


def columns_onehot(row, target_ref, first):
    tall = jnp.broadcast_to(row.astype(jnp.float32), (LANES, row.shape[1]))
    column = jnp.transpose(tall).astype(jnp.int32)
    lower = onehot(iota(column.shape, 1) == (column & (LANES - 1)))
    upper = lax.shift_right_arithmetic(column, log2(LANES)).astype(jnp.bfloat16)
    zero = jnp.zeros_like(lower)
    for m in range(target_ref.shape[1] // LANES):
        target_ref[first : first + row.shape[1], m * LANES : (m + 1) * LANES] = jnp.where(
            upper == jnp.bfloat16(m), lower, zero
        )


def weights_of(logits, half_scale, half_offset, wanted, shift):
    hit = iota(logits.shape, 0) + shift == wanted
    base = jnp.where(hit, -0.5, 0.5)
    return (0.5 * jnp.tanh(logits * half_scale + half_offset) + base).astype(jnp.bfloat16)


def unpack_kernel(
    block,
    odd_ref,
    got_ref,
    spec_cross,
    spec_own,
    spec_partner,
    table_ref,
    slot_ref,
    spec_ref,
    cross_ref,
    partner_ref,
    lower_ref,
    spec_sems,
    sems,
):
    chunks = got_ref.shape[0] // CHUNK
    dev_rows = SB * TILE_ROWS
    odd = odd_ref[0]
    slots = (2 * odd, 1, 2 - 2 * odd)
    loads = [
        pltpu.make_async_copy(
            spec,
            spec_ref.at[pl.ds(pl.multiple_of(slots[n] * dev_rows, dev_rows), dev_rows)],
            spec_sems.at[n],
        )
        for n, spec in enumerate((spec_cross, spec_own, spec_partner))
    ]
    for load in loads:
        load.start()

    lane = iota((CHUNK, CHUNK), 1)
    tail = iota((CHUNK, CHUNK), 0) == lane - (lane & (block - 1)) + (block - 1)
    uppers = []
    for q in range(chunks):
        part = got_ref[q * CHUNK : (q + 1) * CHUNK, :].astype(jnp.float32)
        high = jnp.sum(jnp.where(tail, part[:, :CHUNK], 0.0), axis=0, keepdims=True)
        low = jnp.sum(jnp.where(tail, part[:, CHUNK:], 0.0), axis=0, keepdims=True)
        slot = (high * BASE + low).astype(jnp.int32) - 1
        slot_ref[q : q + 1, :] = slot
        span = slice(q * CHUNK, (q + 1) * CHUNK)
        lower_ref[:, span] = onehot(iota((CHUNK, CHUNK), 0) == (slot & (CHUNK - 1)))
        uppers.append(lax.shift_right_arithmetic(slot, log2(CHUNK)))
    upper = jnp.concatenate(uppers, axis=1)

    edge = EDGE * TILE_ROWS
    for half in range(TILE_DEV // EDGE):
        pick = jnp.concatenate(
            [lower_ref[...] * onehot(upper == half * EDGE + e) for e in range(EDGE)], axis=0
        )
        half_table = matmul(pick, got_ref[...]).astype(jnp.bfloat16)
        table_ref[half * edge : (half + 1) * edge, :] = half_table

    here = pl.multiple_of(odd * edge, edge)
    there = pl.multiple_of(edge - here, edge)
    stores = [
        pltpu.make_async_copy(table_ref.at[pl.ds(here, edge)], cross_ref, sems.at[0]),
        pltpu.make_async_copy(table_ref.at[pl.ds(there, edge)], partner_ref, sems.at[1]),
    ]
    for store in stores:
        store.start()
    for copy in stores + loads:
        copy.wait()


def unpack(odd, got, spectra, block):
    slots, width = got.shape
    rows = TILE_DEV * TILE_ROWS
    chunks = slots // CHUNK
    assert TILE_DEV == 2 * EDGE and CHUNK == TILE_ROWS
    half = pltpu.HBM((rows // 2, width), jnp.bfloat16)
    return pl.pallas_call(
        functools.partial(unpack_kernel, block),
        in_specs=[IN_SMEM, IN_VMEM] + [ANYWHERE] * 3,
        out_specs=[IN_VMEM] * 3 + [IN_HBM] * 2,
        out_shape=[
            jax.ShapeDtypeStruct((rows, width), jnp.bfloat16),
            jax.ShapeDtypeStruct((chunks, CHUNK), jnp.int32),
            jax.ShapeDtypeStruct((3 * SB * TILE_ROWS, width), jnp.bfloat16),
            half,
            half,
        ],
        scratch_shapes=[
            pltpu.VMEM((CHUNK, slots), jnp.bfloat16),
            pltpu.SemaphoreType.DMA((3,)),
            pltpu.SemaphoreType.DMA((2,)),
        ],
        compiler_params=PARAMS,
        name="unpack",
    )(odd, got, *map(in_hbm, spectra))


def tiles_kernel(
    scale_ref,
    bias_ref,
    table_ref,
    slot_ref,
    spec_ref,
    info_prev,
    info_own,
    info_next,
    band_prev,
    band_own,
    band_next,
    back_ref,
    mask_ref,
    weight_ref,
    grad_ref,
    rows_ref,
    sems,
):
    chunks = slot_ref.shape[0]
    dev_rows = SB * TILE_ROWS
    scaling = scale_ref[0] * (1.0 / math.sqrt(table_ref.shape[1]))
    infos = (info_prev, info_own, info_next)
    bands = (band_prev, band_own, band_next)

    edge = EDGE * TILE_ROWS
    for upper in range(TILE_DEV // EDGE):
        pair = table_ref[upper * edge : (upper + 1) * edge, :]
        for source in (upper, upper + 1):
            for k in range(SB):
                first = (source * SB + k) * TILE_ROWS
                column = first - upper * dev_rows
                logits = matmul(pair, spec_ref[first : first + TILE_ROWS, :], ((1,), (1,)))
                for e in range(EDGE):
                    tag = upper * EDGE + e + (EDGE + TILE_DEV * (1 - source) + 1)
                    place = jnp.int32(-1)
                    for j in range(NB):
                        place = jnp.where(bands[source][SB + k, j] == tag, j, place)
                    active = place >= 0
                    span = slice(e * TILE_ROWS, (e + 1) * TILE_ROWS)
                    weight_ref[span, column : column + TILE_ROWS] = weights_of(
                        logits[span, :],
                        jnp.where(active, 0.5 * scaling, 0.0),
                        jnp.where(active, 0.5 * bias_ref[0], -1e30),
                        infos[source][k : k + 1, :],
                        jnp.where(active, place, 2 * NB) * TILE_ROWS,
                    )
        total = matmul(weight_ref[...], spec_ref[upper * dev_rows : (upper + 2) * dev_rows, :])
        grad_ref[upper * edge : (upper + 1) * edge, :] = (scaling * total).astype(jnp.bfloat16)

    def back_step(q, carry):
        for g in range(GROUP):
            columns_onehot(slot_ref[pl.ds(q * GROUP + g, 1), :], mask_ref, g * CHUNK)
        start = pl.multiple_of(q * WIDE, WIDE)
        rows_ref[pl.ds(start, WIDE), :] = matmul(mask_ref[...], grad_ref[...]).astype(jnp.bfloat16)
        chunk_copy(rows_ref, back_ref, sems, q).start()
        return carry

    lax.fori_loop(0, chunks // GROUP, back_step, 0)
    for q in range(chunks // GROUP):
        chunk_copy(rows_ref, back_ref, sems, q).wait()


def tiles(scale, bias, table, slot, spectra, infos):
    rows, width = table.shape
    chunks = slot.shape[0]
    slots = chunks * CHUNK
    return pl.pallas_call(
        tiles_kernel,
        in_specs=[IN_SMEM] * 2 + [IN_VMEM] * 6 + [IN_SMEM] * 3,
        out_specs=IN_HBM,
        out_shape=pltpu.HBM((slots, width), jnp.bfloat16),
        scratch_shapes=[
            pltpu.VMEM((WIDE, rows), jnp.bfloat16),
            pltpu.VMEM((EDGE * TILE_ROWS, 2 * SB * TILE_ROWS), jnp.bfloat16),
            pltpu.VMEM((rows, width), jnp.bfloat16),
            pltpu.VMEM((slots, width), jnp.bfloat16),
            pltpu.SemaphoreType.DMA((chunks,)),
        ],
        compiler_params=PARAMS,
        name="tiles",
    )(scale, bias, table, slot, spectra, *infos, *infos)


def spectra_kernel(
    scale_ref, bias_ref, odd_ref, band_ref, cross_ref, own_ref, partner_ref, spec_ref, info_ref,
    out_ref, ext_ref, sems,
):
    k = pl.program_id(0)
    edge = EDGE * TILE_ROWS
    scaling = scale_ref[0] * (1.0 / math.sqrt(out_ref.shape[1]))

    @pl.when(k == 0)
    def _():
        mine = TILE_DEV * TILE_ROWS
        low = pl.multiple_of(odd_ref[0] * (edge + mine), edge)
        high = pl.multiple_of(edge + mine - low, edge)
        copies = [
            pltpu.make_async_copy(cross_ref, ext_ref.at[pl.ds(low, edge)], sems.at[0]),
            pltpu.make_async_copy(own_ref, ext_ref.at[pl.ds(edge, mine)], sems.at[1]),
            pltpu.make_async_copy(partner_ref, ext_ref.at[pl.ds(high, edge)], sems.at[2]),
        ]
        for copy in copies:
            copy.start()
        for copy in copies:
            copy.wait()

    total = jnp.zeros(out_ref.shape, jnp.float32)
    for j in range(NB):
        start = pl.multiple_of((band_ref[SB + k, j] - 1) * TILE_ROWS, TILE_ROWS)
        tile = ext_ref[pl.ds(start, TILE_ROWS), :]
        weights = weights_of(
            matmul(tile, spec_ref[...], ((1,), (1,))),
            0.5 * scaling,
            0.5 * bias_ref[0],
            info_ref[pl.ds(k, 1), :],
            j * TILE_ROWS,
        )
        total += matmul(weights, tile, ((0,), (0,)))
    out_ref[...] = (scaling * total).astype(jnp.bfloat16)


def spectra_gradient(scale, bias, odd, info, cross, table, partner, spectra):
    width = spectra.shape[1]
    edge = EDGE * TILE_ROWS
    return pl.pallas_call(
        spectra_kernel,
        grid=(SB,),
        in_specs=[
            IN_SMEM,
            IN_SMEM,
            IN_SMEM,
            IN_SMEM,
            ANYWHERE,
            ANYWHERE,
            ANYWHERE,
            pl.BlockSpec((TILE_ROWS, width), lambda k: (k, 0)),
            pl.BlockSpec((2 * SB, TILE_ROWS), lambda k: (0, 0)),
        ],
        out_specs=pl.BlockSpec((TILE_ROWS, width), lambda k: (k, 0)),
        scratch_shapes=[
            pltpu.VMEM((4 * edge, width), jnp.bfloat16),
            pltpu.SemaphoreType.DMA((3,)),
        ],
        compiler_params=PARAMS,
        out_shape=jax.ShapeDtypeStruct((SB * TILE_ROWS, width), jnp.bfloat16),
        name="spectra_gradient",
    )(scale, bias, odd, info, cross, table, partner, spectra, info)


def home_kernel(pos_ref, got_ref, out_ref, pick_ref, grad_ref, sems):
    chunks = pos_ref.shape[0]

    def chunk(c, carry):
        for g in range(GROUP):
            columns_onehot(pos_ref[pl.ds(c * GROUP + g, 1), :], pick_ref, g * CHUNK)
        grad = matmul(pick_ref[...], got_ref[...]).astype(jnp.bfloat16)
        grad_ref[pl.ds(pl.multiple_of(c * WIDE, WIDE), WIDE), :] = grad
        chunk_copy(grad_ref, out_ref, sems, c).start()
        return carry

    lax.fori_loop(0, chunks // GROUP, chunk, 0)
    for c in range(chunks // GROUP):
        chunk_copy(grad_ref, out_ref, sems, c).wait()


def home(position, returned):
    slots, width = returned.shape
    chunks = position.shape[0]
    rows = chunks * CHUNK
    return pl.pallas_call(
        home_kernel,
        in_specs=[IN_VMEM] * 2,
        out_specs=IN_HBM,
        out_shape=jax.ShapeDtypeStruct((rows, width), jnp.bfloat16),
        scratch_shapes=[
            pltpu.VMEM((WIDE, slots), jnp.bfloat16),
            pltpu.VMEM((rows, width), jnp.bfloat16),
            pltpu.SemaphoreType.DMA((chunks,)),
        ],
        compiler_params=PARAMS,
        name="home",
    )(position, returned)


def from_partner(value):
    count = lax.axis_size("mass") * lax.axis_size("prot")
    return lax.ppermute(value, AXES, [(i, i ^ 1) for i in range(count)])


def from_cross(value):
    count = lax.axis_size("mass") * lax.axis_size("prot")
    pairs = [(i, i + 1) for i in range(1, count - 1, 2)]
    return lax.ppermute(value, AXES, pairs + [(j, i) for i, j in pairs])


def program(spectra, peptides, destination, band, positive, logit_scale, logit_bias):
    devices = lax.axis_size("mass") * lax.axis_size("prot")
    rows = peptides.shape[0]
    block = 2 * (rows // devices)

    assert devices % 2 == 0
    odd = (lax.axis_index(AXES) & 1).reshape(1)
    spec_cross = from_cross(spectra)
    spec_partner = from_partner(spectra)
    send, position, info = pack(destination, peptides, positive, band, devices, block)
    info_cross = from_cross(info)
    info_partner = from_partner(info)
    info_prev = jnp.where(odd == 1, info_partner, info_cross)
    info_next = jnp.where(odd == 1, info_cross, info_partner)
    got = lax.all_to_all(send, AXES, 0, 0, tiled=True)
    table, slot, specs, to_cross, to_partner = unpack(
        odd, got, (spec_cross, spectra, spec_partner), block
    )
    cross = from_cross(to_cross)
    partner = from_partner(to_partner)
    back = tiles(logit_scale, logit_bias, table, slot, specs, (info_prev, info, info_next))
    returned = lax.all_to_all(back, AXES, 0, 0, tiled=True)
    spec_grad = spectra_gradient(
        logit_scale, logit_bias, odd, info, cross, table, partner, spectra
    )
    return (spec_grad, home(position, returned))


def solution(mesh):
    in_specs = (
        P(AXES, None),
        P(AXES, None),
        P(AXES),
        P(AXES, None),
        P(AXES),
        P(),
        P(),
    )
    out_specs = (P(AXES, None), P(AXES, None))
    return jax.shard_map(program, mesh=mesh, in_specs=in_specs, out_specs=out_specs, check_vma=False)
```

```python
import functools
import math

import jax
import jax.numpy as jnp
from jax import lax
from jax.experimental import pallas as pl
from jax.experimental.pallas import tpu as pltpu
from jax.sharding import PartitionSpec as P


TILE_ROWS = 256
EDGE = 2
NB = 6
TILE_DEV = 4
SB = 4
CHUNK = 256
AXES = ("mass", "prot")
BASE = 256
GROUP = 2
WIDE = GROUP * CHUNK
LANES = 128
VMEM_LIMIT = 24 * 1024 * 1024
PARAMS = pltpu.CompilerParams(vmem_limit_bytes=VMEM_LIMIT)
IN_VMEM = pl.BlockSpec(memory_space=pltpu.VMEM)
IN_SMEM = pl.BlockSpec(memory_space=pltpu.SMEM)
ANYWHERE = pl.BlockSpec(memory_space=pl.ANY)
IN_HBM = pl.BlockSpec(memory_space=pltpu.HBM)


def log2(value):
    bits = value.bit_length() - 1
    assert value == 1 << bits
    return bits


def iota(shape, dim):
    return lax.broadcasted_iota(jnp.int32, shape, dim)


def onehot(mask):
    return jnp.where(mask, 1.0, 0.0).astype(jnp.bfloat16)


def matmul(a, b, dims=((1,), (0,))):
    return lax.dot_general(a, b, (dims, ((), ())), preferred_element_type=jnp.float32)


def chunk_copy(source, target, sems, c):
    part = pl.ds(pl.multiple_of(c * WIDE, WIDE), WIDE)
    return pltpu.make_async_copy(source.at[part], target.at[part], sems.at[c])


def in_hbm(value):
    return pltpu.with_memory_space_constraint(value, pltpu.HBM)


def pack_kernel(
    devices,
    block,
    dest_any,
    pep_any,
    want_any,
    band_any,
    send_ref,
    pos_ref,
    info_ref,
    dest_ref,
    pep_ref,
    want_ref,
    band_ref,
    meta_ref,
    lower_ref,
    upper_ref,
    rows_ref,
    load_sems,
    sems,
):
    rows = pep_ref.shape[0]
    pairs = [(dest_any, dest_ref), (want_any, want_ref), (band_any, band_ref), (pep_any, pep_ref)]
    loads = [pltpu.make_async_copy(*pair, load_sems.at[n]) for n, pair in enumerate(pairs)]
    for load in loads:
        load.start()
    for load in loads[:3]:
        load.wait()
    info_ref[...] = jnp.zeros_like(info_ref)
    for k in range(SB):
        info_ref[k : k + 1, :] = want_ref[k]
    info_ref[SB:, :NB] = band_ref[...] + 1

    dest = dest_ref[...]
    owner = lax.shift_right_logical(dest, log2(rows))
    filled = dest - owner * rows + 1
    member = iota((devices, rows), 0) == owner
    groups = [
        jnp.where(member[:, g : g + LANES], 1.0, 0.0) for g in range(0, rows, LANES)
    ]
    earlier = onehot(iota((LANES, LANES), 0) < iota((LANES, LANES), 1))
    seen = []
    count = jnp.zeros((devices, 1), jnp.float32)
    for group in groups:
        inside = matmul(group.astype(jnp.bfloat16), earlier) + count
        seen.append(jnp.sum(group * inside, axis=0, keepdims=True))
        count = count + jnp.sum(group, axis=1, keepdims=True)
    rank = jnp.concatenate(seen, axis=1).astype(jnp.int32)
    position = owner * block + rank
    for c in range(rows // CHUNK):
        pos_ref[c : c + 1, :] = position[:, c * CHUNK : (c + 1) * CHUNK]
    high = lax.shift_right_logical(filled, log2(BASE))
    low = filled - high * BASE
    lane = iota((2 * CHUNK, rows), 0)
    part = jnp.where(lane < CHUNK, high.astype(jnp.float32), low.astype(jnp.float32))
    spread = jnp.where((lane & (block - 1)) == rank, part, 0.0).astype(jnp.bfloat16)
    meta_ref[...] = matmul(onehot(member), spread, ((1,), (1,))).astype(jnp.bfloat16)
    lower_ref[...] = onehot(iota((CHUNK, rows), 0) == (position & (CHUNK - 1)))
    upper_ref[...] = lax.shift_right_logical(position, log2(CHUNK))
    loads[3].wait()

    for c in range(send_ref.shape[0] // WIDE):
        base = c * WIDE
        pick = jnp.concatenate(
            [lower_ref[...] * onehot(upper_ref[...] == c * GROUP + g) for g in range(GROUP)], axis=0
        )
        tail = onehot(
            iota((WIDE, devices), 0) + base == iota((WIDE, devices), 1) * block + (block - 1)
        )
        sent = matmul(pick, pep_ref[...]) + matmul(tail, meta_ref[...])
        rows_ref[base : base + WIDE, :] = sent.astype(jnp.bfloat16)
        chunk_copy(rows_ref, send_ref, sems, c).start()
    for c in range(send_ref.shape[0] // WIDE):
        chunk_copy(rows_ref, send_ref, sems, c).wait()


def pack(destination, peptides, positive, band, devices, block):
    rows, width = peptides.shape
    slots = devices * block
    operands = (
        destination.reshape(1, rows), peptides, positive.reshape(SB, 1, TILE_ROWS), band
    )
    assert width == 2 * CHUNK and CHUNK % block == 0 and slots % WIDE == 0
    return pl.pallas_call(
        functools.partial(pack_kernel, devices, block),
        in_specs=[IN_HBM] * 4,
        out_specs=[IN_HBM, IN_VMEM, IN_VMEM],
        out_shape=[
            pltpu.HBM((slots, width), jnp.bfloat16),
            jax.ShapeDtypeStruct((rows // CHUNK, CHUNK), jnp.int32),
            jax.ShapeDtypeStruct((2 * SB, TILE_ROWS), jnp.int32),
        ],
        scratch_shapes=[
            pltpu.VMEM((1, rows), jnp.int32),
            pltpu.VMEM((rows, width), jnp.bfloat16),
            pltpu.VMEM((SB, 1, TILE_ROWS), jnp.int32),
            pltpu.VMEM((SB, NB), jnp.int32),
            pltpu.VMEM((devices, width), jnp.bfloat16),
            pltpu.VMEM((CHUNK, rows), jnp.bfloat16),
            pltpu.VMEM((1, rows), jnp.int32),
            pltpu.VMEM((slots, width), jnp.bfloat16),
            pltpu.SemaphoreType.DMA((4,)),
            pltpu.SemaphoreType.DMA((slots // WIDE,)),
        ],
        compiler_params=PARAMS,
        name="pack",
    )(*map(in_hbm, operands))


def columns_onehot(row, target_ref, first):
    tall = jnp.broadcast_to(row.astype(jnp.float32), (LANES, row.shape[1]))
    column = jnp.transpose(tall).astype(jnp.int32)
    lower = onehot(iota(column.shape, 1) == (column & (LANES - 1)))
    upper = lax.shift_right_arithmetic(column, log2(LANES)).astype(jnp.bfloat16)
    zero = jnp.zeros_like(lower)
    for m in range(target_ref.shape[1] // LANES):
        target_ref[first : first + row.shape[1], m * LANES : (m + 1) * LANES] = jnp.where(
            upper == jnp.bfloat16(m), lower, zero
        )


def doubled_weights(logits, half_scale, half_offset, wanted, shift):
    hit = iota(logits.shape, 0) + shift == wanted
    base = jnp.where(hit, -1.0, 1.0)
    return (jnp.tanh(logits * half_scale + half_offset) + base).astype(jnp.bfloat16)


def unpack_kernel(
    block,
    odd_ref,
    got_ref,
    table_ref,
    slot_ref,
    cross_ref,
    partner_ref,
    lower_ref,
    sems,
):
    chunks = got_ref.shape[0] // CHUNK
    odd = odd_ref[0]

    lane = iota((CHUNK, CHUNK), 1)
    tail = iota((CHUNK, CHUNK), 0) == lane - (lane & (block - 1)) + (block - 1)
    uppers = []
    for q in range(chunks):
        part = got_ref[q * CHUNK : (q + 1) * CHUNK, :].astype(jnp.float32)
        high = jnp.sum(jnp.where(tail, part[:, :CHUNK], 0.0), axis=0, keepdims=True)
        low = jnp.sum(jnp.where(tail, part[:, CHUNK:], 0.0), axis=0, keepdims=True)
        slot = (high * BASE + low).astype(jnp.int32) - 1
        slot_ref[q : q + 1, :] = slot
        span = slice(q * CHUNK, (q + 1) * CHUNK)
        lower_ref[:, span] = onehot(iota((CHUNK, CHUNK), 0) == (slot & (CHUNK - 1)))
        uppers.append(lax.shift_right_arithmetic(slot, log2(CHUNK)))
    upper = jnp.concatenate(uppers, axis=1)

    edge = EDGE * TILE_ROWS
    for half in range(TILE_DEV // EDGE):
        pick = jnp.concatenate(
            [lower_ref[...] * onehot(upper == half * EDGE + e) for e in range(EDGE)], axis=0
        )
        half_table = matmul(pick, got_ref[...]).astype(jnp.bfloat16)
        table_ref[half * edge : (half + 1) * edge, :] = half_table

    here = pl.multiple_of(odd * edge, edge)
    there = pl.multiple_of(edge - here, edge)
    stores = [
        pltpu.make_async_copy(table_ref.at[pl.ds(here, edge)], cross_ref, sems.at[0]),
        pltpu.make_async_copy(table_ref.at[pl.ds(there, edge)], partner_ref, sems.at[1]),
    ]
    for store in stores:
        store.start()
    for store in stores:
        store.wait()


def unpack(odd, got, block):
    slots, width = got.shape
    rows = TILE_DEV * TILE_ROWS
    chunks = slots // CHUNK
    assert TILE_DEV == 2 * EDGE and CHUNK == TILE_ROWS
    half = pltpu.HBM((rows // 2, width), jnp.bfloat16)
    return pl.pallas_call(
        functools.partial(unpack_kernel, block),
        in_specs=[IN_SMEM, IN_VMEM],
        out_specs=[IN_VMEM] * 2 + [IN_HBM] * 2,
        out_shape=[
            jax.ShapeDtypeStruct((rows, width), jnp.bfloat16),
            jax.ShapeDtypeStruct((chunks, CHUNK), jnp.int32),
            half,
            half,
        ],
        scratch_shapes=[
            pltpu.VMEM((CHUNK, slots), jnp.bfloat16),
            pltpu.SemaphoreType.DMA((2,)),
        ],
        compiler_params=PARAMS,
        name="unpack",
    )(odd, got)


def tiles_kernel(
    scale_ref,
    bias_ref,
    odd_ref,
    table_ref,
    slot_ref,
    spec_own,
    info_own,
    band_own,
    spec_cross,
    spec_partner,
    info_cross,
    info_partner,
    back_ref,
    mask_ref,
    weight_ref,
    grad_ref,
    side_ref,
    info_ref,
    band_ref,
    rows_ref,
    load_sems,
    sems,
):
    chunks = slot_ref.shape[0]
    dev_rows = SB * TILE_ROWS
    edge = EDGE * TILE_ROWS
    scaling = scale_ref[0] * (1.0 / math.sqrt(table_ref.shape[1]))
    odd = odd_ref[0]
    loads = []
    sides = [(odd, spec_cross, info_cross), (1 - odd, spec_partner, info_partner)]
    for n, (side, spec, info) in enumerate(sides):
        big = pl.ds(pl.multiple_of(side * dev_rows, dev_rows), dev_rows)
        loads += [
            pltpu.make_async_copy(spec, side_ref.at[big], load_sems.at[n, 0]),
            pltpu.make_async_copy(info, info_ref.at[side], load_sems.at[n, 1]),
            pltpu.make_async_copy(info, band_ref.at[side], load_sems.at[n, 2]),
        ]
    for load in loads:
        load.start()
    specs = (side_ref.at[pl.ds(0, dev_rows)], spec_own, side_ref.at[pl.ds(dev_rows, dev_rows)])
    infos = (info_ref.at[0], info_own, info_ref.at[1])
    bands = (band_ref.at[0], band_own, band_ref.at[1])

    def weigh(upper, source):
        pair = table_ref[upper * edge : (upper + 1) * edge, :]
        for k in range(SB):
            column = ((source - upper) * SB + k) * TILE_ROWS
            block = specs[source][k * TILE_ROWS : (k + 1) * TILE_ROWS, :]
            logits = matmul(pair, block, ((1,), (1,)))
            for e in range(EDGE):
                tag = upper * EDGE + e + (EDGE + TILE_DEV * (1 - source) + 1)
                place = jnp.int32(-1)
                for j in range(NB):
                    place = jnp.where(bands[source][SB + k, j] == tag, j, place)
                active = place >= 0
                span = slice(e * TILE_ROWS, (e + 1) * TILE_ROWS)
                weight_ref[upper, span, column : column + TILE_ROWS] = doubled_weights(
                    logits[span, :],
                    jnp.where(active, 0.5 * scaling, 0.0),
                    jnp.where(active, 0.5 * bias_ref[0], -1e30),
                    infos[source][k : k + 1, :],
                    jnp.where(active, place, 2 * NB) * TILE_ROWS,
                )

    def reduce(upper):
        total = matmul(weight_ref[upper, :, :dev_rows], specs[upper][...])
        total += matmul(weight_ref[upper, :, dev_rows:], specs[upper + 1][...])
        grad_ref[upper * edge : (upper + 1) * edge, :] = (0.5 * scaling * total).astype(
            jnp.bfloat16
        )

    weigh(0, 1)
    weigh(1, 1)
    for load in loads:
        load.wait()
    weigh(0, 0)
    reduce(0)
    weigh(1, 2)
    reduce(1)

    def back_step(q, carry):
        for g in range(GROUP):
            columns_onehot(slot_ref[pl.ds(q * GROUP + g, 1), :], mask_ref, g * CHUNK)
        back = matmul(mask_ref[...], grad_ref[...])
        start = pl.multiple_of(q * WIDE, WIDE)
        rows_ref[pl.ds(start, WIDE), :] = back.astype(jnp.bfloat16)
        chunk_copy(rows_ref, back_ref, sems, q).start()
        return carry

    lax.fori_loop(0, chunks // GROUP, back_step, 0)
    for q in range(chunks // GROUP):
        chunk_copy(rows_ref, back_ref, sems, q).wait()


def tiles(scale, bias, odd, table, slot, spectra, info, others):
    rows, width = table.shape
    chunks = slot.shape[0]
    slots = chunks * CHUNK
    return pl.pallas_call(
        tiles_kernel,
        in_specs=[IN_SMEM] * 3 + [IN_VMEM] * 4 + [IN_SMEM] + [ANYWHERE] * 4,
        out_specs=IN_HBM,
        out_shape=pltpu.HBM((slots, width), jnp.bfloat16),
        scratch_shapes=[
            pltpu.VMEM((WIDE, rows), jnp.bfloat16),
            pltpu.VMEM((2, EDGE * TILE_ROWS, 2 * SB * TILE_ROWS), jnp.bfloat16),
            pltpu.VMEM((rows, width), jnp.bfloat16),
            pltpu.VMEM((2 * SB * TILE_ROWS, width), jnp.bfloat16),
            pltpu.VMEM((2, 2 * SB, TILE_ROWS), jnp.int32),
            pltpu.SMEM((2, 2 * SB, TILE_ROWS), jnp.int32),
            pltpu.VMEM((slots, width), jnp.bfloat16),
            pltpu.SemaphoreType.DMA((2, 3)),
            pltpu.SemaphoreType.DMA((chunks // GROUP,)),
        ],
        compiler_params=PARAMS,
        name="tiles",
    )(scale, bias, odd, table, slot, spectra, info, info, *map(in_hbm, others[:2]), *others[2:])


def spectra_kernel(
    scale_ref, bias_ref, odd_ref, band_ref, cross_ref, own_ref, partner_ref, spec_ref, info_ref,
    out_ref, ext_ref, sems,
):
    k = pl.program_id(0)
    edge = EDGE * TILE_ROWS
    scaling = scale_ref[0] * (1.0 / math.sqrt(out_ref.shape[1]))

    @pl.when(k == 0)
    def _():
        mine = TILE_DEV * TILE_ROWS
        low = pl.multiple_of(odd_ref[0] * (edge + mine), edge)
        high = pl.multiple_of(edge + mine - low, edge)
        copies = [
            pltpu.make_async_copy(cross_ref, ext_ref.at[pl.ds(low, edge)], sems.at[0]),
            pltpu.make_async_copy(own_ref, ext_ref.at[pl.ds(edge, mine)], sems.at[1]),
            pltpu.make_async_copy(partner_ref, ext_ref.at[pl.ds(high, edge)], sems.at[2]),
        ]
        for copy in copies:
            copy.start()
        for copy in copies:
            copy.wait()

    total = jnp.zeros(out_ref.shape, jnp.float32)
    for j in range(NB):
        start = pl.multiple_of((band_ref[SB + k, j] - 1) * TILE_ROWS, TILE_ROWS)
        tile = ext_ref[pl.ds(start, TILE_ROWS), :]
        weights = doubled_weights(
            matmul(tile, spec_ref[...], ((1,), (1,))),
            0.5 * scaling,
            0.5 * bias_ref[0],
            info_ref[pl.ds(k, 1), :],
            j * TILE_ROWS,
        )
        total += matmul(weights, tile, ((0,), (0,)))
    out_ref[...] = (0.5 * scaling * total).astype(jnp.bfloat16)


def spectra_gradient(scale, bias, odd, info, cross, table, partner, spectra):
    width = spectra.shape[1]
    edge = EDGE * TILE_ROWS
    return pl.pallas_call(
        spectra_kernel,
        grid=(SB,),
        in_specs=[
            IN_SMEM,
            IN_SMEM,
            IN_SMEM,
            IN_SMEM,
            ANYWHERE,
            ANYWHERE,
            ANYWHERE,
            pl.BlockSpec((TILE_ROWS, width), lambda k: (k, 0)),
            pl.BlockSpec((2 * SB, TILE_ROWS), lambda k: (0, 0)),
        ],
        out_specs=pl.BlockSpec((TILE_ROWS, width), lambda k: (k, 0)),
        scratch_shapes=[
            pltpu.VMEM((4 * edge, width), jnp.bfloat16),
            pltpu.SemaphoreType.DMA((3,)),
        ],
        compiler_params=PARAMS,
        out_shape=jax.ShapeDtypeStruct((SB * TILE_ROWS, width), jnp.bfloat16),
        name="spectra_gradient",
    )(scale, bias, odd, info, cross, table, partner, spectra, info)


def home_kernel(pos_ref, got_ref, out_ref, pick_ref, grad_ref, sems):
    chunks = pos_ref.shape[0]
    for c in range(chunks // GROUP):
        pick = pick_ref.at[c % 2]
        for g in range(GROUP):
            columns_onehot(pos_ref[c * GROUP + g : c * GROUP + g + 1, :], pick, g * CHUNK)
        grad = matmul(pick[...], got_ref[...])
        grad_ref[c * WIDE : (c + 1) * WIDE, :] = grad.astype(jnp.bfloat16)
        chunk_copy(grad_ref, out_ref, sems, c).start()
    for c in range(chunks // GROUP):
        chunk_copy(grad_ref, out_ref, sems, c).wait()


def home(position, returned):
    slots, width = returned.shape
    chunks = position.shape[0]
    rows = chunks * CHUNK
    return pl.pallas_call(
        home_kernel,
        in_specs=[IN_VMEM] * 2,
        out_specs=IN_HBM,
        out_shape=jax.ShapeDtypeStruct((rows, width), jnp.bfloat16),
        scratch_shapes=[
            pltpu.VMEM((2, WIDE, slots), jnp.bfloat16),
            pltpu.VMEM((rows, width), jnp.bfloat16),
            pltpu.SemaphoreType.DMA((chunks,)),
        ],
        compiler_params=PARAMS,
        name="home",
    )(position, returned)


def from_partner(value):
    count = lax.axis_size("mass") * lax.axis_size("prot")
    return lax.ppermute(value, AXES, [(i, i ^ 1) for i in range(count)])


def from_cross(value):
    count = lax.axis_size("mass") * lax.axis_size("prot")
    pairs = [(i, i + 1) for i in range(1, count - 1, 2)]
    return lax.ppermute(value, AXES, pairs + [(j, i) for i, j in pairs])


def program(spectra, peptides, destination, band, positive, logit_scale, logit_bias):
    devices = lax.axis_size("mass") * lax.axis_size("prot")
    rows = peptides.shape[0]
    block = 2 * (rows // devices)

    assert devices % 2 == 0
    odd = (lax.axis_index(AXES) & 1).reshape(1)
    spec_cross = from_cross(spectra)
    spec_partner = from_partner(spectra)
    send, position, info = pack(destination, peptides, positive, band, devices, block)
    info_cross = from_cross(info)
    info_partner = from_partner(info)
    got = lax.all_to_all(send, AXES, 0, 0, tiled=True)
    table, slot, to_cross, to_partner = unpack(odd, got, block)
    cross = from_cross(to_cross)
    partner = from_partner(to_partner)
    back = tiles(
        logit_scale, logit_bias, odd, table, slot, spectra, info,
        (spec_cross, spec_partner, info_cross, info_partner),
    )
    returned = lax.all_to_all(back, AXES, 0, 0, tiled=True)
    spec_grad = spectra_gradient(
        logit_scale, logit_bias, odd, info, cross, table, partner, spectra
    )
    return (spec_grad, home(position, returned))


def solution(mesh):
    in_specs = (
        P(AXES, None),
        P(AXES, None),
        P(AXES),
        P(AXES, None),
        P(AXES),
        P(),
        P(),
    )
    out_specs = (P(AXES, None), P(AXES, None))
    return jax.shard_map(program, mesh=mesh, in_specs=in_specs, out_specs=out_specs, check_vma=False)
```

```python
import functools
import math

import jax
import jax.numpy as jnp
from jax import lax
from jax.experimental import pallas as pl
from jax.experimental.pallas import tpu as pltpu
from jax.sharding import PartitionSpec as P


TILE_ROWS = 256
EDGE = 2
NB = 6
TILE_DEV = 4
SB = 4
CHUNK = 256
AXES = ("mass", "prot")
BASE = 256
GROUP = 2
WIDE = GROUP * CHUNK
LANES = 128
VMEM_LIMIT = 24 * 1024 * 1024
PARAMS = pltpu.CompilerParams(vmem_limit_bytes=VMEM_LIMIT)
IN_VMEM = pl.BlockSpec(memory_space=pltpu.VMEM)
IN_SMEM = pl.BlockSpec(memory_space=pltpu.SMEM)
ANYWHERE = pl.BlockSpec(memory_space=pl.ANY)
IN_HBM = pl.BlockSpec(memory_space=pltpu.HBM)


def log2(value):
    bits = value.bit_length() - 1
    assert value == 1 << bits
    return bits


def iota(shape, dim):
    return lax.broadcasted_iota(jnp.int32, shape, dim)


def onehot(mask):
    return jnp.where(mask, 1.0, 0.0).astype(jnp.bfloat16)


def matmul(a, b, dims=((1,), (0,))):
    return lax.dot_general(a, b, (dims, ((), ())), preferred_element_type=jnp.float32)


def chunk_copy(source, target, sems, c):
    part = pl.ds(pl.multiple_of(c * WIDE, WIDE), WIDE)
    return pltpu.make_async_copy(source.at[part], target.at[part], sems.at[c])


def in_hbm(value):
    return pltpu.with_memory_space_constraint(value, pltpu.HBM)


def pack_kernel(
    devices,
    block,
    dest_any,
    pep_any,
    want_any,
    band_any,
    send_ref,
    pos_ref,
    info_ref,
    dest_ref,
    pep_ref,
    want_ref,
    band_ref,
    meta_ref,
    lower_ref,
    upper_ref,
    rows_ref,
    load_sems,
    sems,
):
    rows = pep_ref.shape[0]
    pairs = [(dest_any, dest_ref), (want_any, want_ref), (band_any, band_ref), (pep_any, pep_ref)]
    loads = [pltpu.make_async_copy(*pair, load_sems.at[n]) for n, pair in enumerate(pairs)]
    for load in loads:
        load.start()
    for load in loads[:3]:
        load.wait()
    info_ref[...] = jnp.zeros_like(info_ref)
    for k in range(SB):
        info_ref[k : k + 1, :] = want_ref[k]
    info_ref[SB:, :NB] = band_ref[...] + 1

    dest = dest_ref[...]
    owner = lax.shift_right_logical(dest, log2(rows))
    filled = dest - owner * rows + 1
    member = iota((devices, rows), 0) == owner
    groups = [
        jnp.where(member[:, g : g + LANES], 1.0, 0.0) for g in range(0, rows, LANES)
    ]
    earlier = onehot(iota((LANES, LANES), 0) < iota((LANES, LANES), 1))
    seen = []
    count = jnp.zeros((devices, 1), jnp.float32)
    for group in groups:
        inside = matmul(group.astype(jnp.bfloat16), earlier) + count
        seen.append(jnp.sum(group * inside, axis=0, keepdims=True))
        count = count + jnp.sum(group, axis=1, keepdims=True)
    rank = jnp.concatenate(seen, axis=1).astype(jnp.int32)
    position = owner * block + rank
    for c in range(rows // CHUNK):
        pos_ref[c : c + 1, :] = position[:, c * CHUNK : (c + 1) * CHUNK]
    high = lax.shift_right_logical(filled, log2(BASE))
    low = filled - high * BASE
    lane = iota((2 * LANES, rows), 0)
    part = jnp.where(lane < LANES, high.astype(jnp.float32), low.astype(jnp.float32))
    spread = jnp.where((lane & (block - 1)) == rank, part, 0.0).astype(jnp.bfloat16)
    meta = matmul(onehot(member), spread, ((1,), (1,))).astype(jnp.bfloat16)
    copies = CHUNK // LANES
    meta_ref[...] = jnp.concatenate([meta[:, :LANES]] * copies + [meta[:, LANES:]] * copies, axis=1)
    lower_ref[...] = onehot(iota((CHUNK, rows), 0) == (position & (CHUNK - 1)))
    upper_ref[...] = lax.shift_right_logical(position, log2(CHUNK))
    loads[3].wait()

    for c in range(send_ref.shape[0] // WIDE):
        base = c * WIDE
        pick = jnp.concatenate(
            [lower_ref[...] * onehot(upper_ref[...] == c * GROUP + g) for g in range(GROUP)], axis=0
        )
        tail = onehot(
            iota((WIDE, devices), 0) + base == iota((WIDE, devices), 1) * block + (block - 1)
        )
        sent = matmul(pick, pep_ref[...]) + matmul(tail, meta_ref[...])
        rows_ref[base : base + WIDE, :] = sent.astype(jnp.bfloat16)
        chunk_copy(rows_ref, send_ref, sems, c).start()
    for c in range(send_ref.shape[0] // WIDE):
        chunk_copy(rows_ref, send_ref, sems, c).wait()


def pack(destination, peptides, positive, band, devices, block):
    rows, width = peptides.shape
    slots = devices * block
    operands = (
        destination.reshape(1, rows), peptides, positive.reshape(SB, 1, TILE_ROWS), band
    )
    assert width == 2 * CHUNK and LANES % block == 0 and slots % WIDE == 0
    return pl.pallas_call(
        functools.partial(pack_kernel, devices, block),
        in_specs=[IN_HBM] * 4,
        out_specs=[IN_HBM, IN_VMEM, IN_VMEM],
        out_shape=[
            pltpu.HBM((slots, width), jnp.bfloat16),
            jax.ShapeDtypeStruct((rows // CHUNK, CHUNK), jnp.int32),
            jax.ShapeDtypeStruct((2 * SB, TILE_ROWS), jnp.int32),
        ],
        scratch_shapes=[
            pltpu.VMEM((1, rows), jnp.int32),
            pltpu.VMEM((rows, width), jnp.bfloat16),
            pltpu.VMEM((SB, 1, TILE_ROWS), jnp.int32),
            pltpu.VMEM((SB, NB), jnp.int32),
            pltpu.VMEM((devices, width), jnp.bfloat16),
            pltpu.VMEM((CHUNK, rows), jnp.bfloat16),
            pltpu.VMEM((1, rows), jnp.int32),
            pltpu.VMEM((slots, width), jnp.bfloat16),
            pltpu.SemaphoreType.DMA((4,)),
            pltpu.SemaphoreType.DMA((slots // WIDE,)),
        ],
        compiler_params=PARAMS,
        name="pack",
    )(*map(in_hbm, operands))


def columns_onehot(row, target_ref, first):
    tall = jnp.broadcast_to(row.astype(jnp.float32), (LANES, row.shape[1]))
    column = jnp.transpose(tall).astype(jnp.int32)
    lower = onehot(iota(column.shape, 1) == (column & (LANES - 1)))
    upper = lax.shift_right_arithmetic(column, log2(LANES)).astype(jnp.bfloat16)
    zero = jnp.zeros_like(lower)
    for m in range(target_ref.shape[1] // LANES):
        target_ref[first : first + row.shape[1], m * LANES : (m + 1) * LANES] = jnp.where(
            upper == jnp.bfloat16(m), lower, zero
        )


def doubled_weights(logits, half_scale, half_offset, wanted, shift):
    hit = iota(logits.shape, 0) + shift == wanted
    base = jnp.where(hit, -1.0, 1.0)
    return (jnp.tanh(logits * half_scale + half_offset) + base).astype(jnp.bfloat16)


def unpack_kernel(
    block,
    odd_ref,
    got_ref,
    table_ref,
    slot_ref,
    cross_ref,
    partner_ref,
    lower_ref,
    sems,
):
    chunks = got_ref.shape[0] // CHUNK
    odd = odd_ref[0]

    lane = iota((CHUNK, CHUNK), 1)
    tail = iota((CHUNK, CHUNK), 0) == lane - (lane & (block - 1)) + (block - 1)
    uppers = []
    for q in range(chunks):
        part = got_ref[q * CHUNK : (q + 1) * CHUNK, :].astype(jnp.float32)
        high = jnp.sum(jnp.where(tail, part[:, :CHUNK], 0.0), axis=0, keepdims=True)
        low = jnp.sum(jnp.where(tail, part[:, CHUNK:], 0.0), axis=0, keepdims=True)
        slot = (high * BASE + low).astype(jnp.int32) - 1
        slot_ref[q : q + 1, :] = slot
        span = slice(q * CHUNK, (q + 1) * CHUNK)
        lower_ref[:, span] = onehot(iota((CHUNK, CHUNK), 0) == (slot & (CHUNK - 1)))
        uppers.append(lax.shift_right_arithmetic(slot, log2(CHUNK)))
    upper = jnp.concatenate(uppers, axis=1)

    edge = EDGE * TILE_ROWS
    for half in range(TILE_DEV // EDGE):
        pick = jnp.concatenate(
            [lower_ref[...] * onehot(upper == half * EDGE + e) for e in range(EDGE)], axis=0
        )
        half_table = matmul(pick, got_ref[...]).astype(jnp.bfloat16)
        table_ref[half * edge : (half + 1) * edge, :] = half_table

    here = pl.multiple_of(odd * edge, edge)
    there = pl.multiple_of(edge - here, edge)
    stores = [
        pltpu.make_async_copy(table_ref.at[pl.ds(here, edge)], cross_ref, sems.at[0]),
        pltpu.make_async_copy(table_ref.at[pl.ds(there, edge)], partner_ref, sems.at[1]),
    ]
    for store in stores:
        store.start()
    for store in stores:
        store.wait()


def unpack(odd, got, block):
    slots, width = got.shape
    rows = TILE_DEV * TILE_ROWS
    chunks = slots // CHUNK
    assert TILE_DEV == 2 * EDGE and CHUNK == TILE_ROWS
    half = pltpu.HBM((rows // 2, width), jnp.bfloat16)
    return pl.pallas_call(
        functools.partial(unpack_kernel, block),
        in_specs=[IN_SMEM, IN_VMEM],
        out_specs=[IN_VMEM] * 2 + [IN_HBM] * 2,
        out_shape=[
            jax.ShapeDtypeStruct((rows, width), jnp.bfloat16),
            jax.ShapeDtypeStruct((chunks, CHUNK), jnp.int32),
            half,
            half,
        ],
        scratch_shapes=[
            pltpu.VMEM((CHUNK, slots), jnp.bfloat16),
            pltpu.SemaphoreType.DMA((2,)),
        ],
        compiler_params=PARAMS,
        name="unpack",
    )(odd, got)


def tiles_kernel(
    scale_ref,
    bias_ref,
    odd_ref,
    table_ref,
    slot_ref,
    spec_own,
    info_own,
    band_own,
    spec_cross,
    spec_partner,
    info_cross,
    info_partner,
    back_ref,
    mask_ref,
    weight_ref,
    grad_ref,
    side_ref,
    info_ref,
    band_ref,
    rows_ref,
    load_sems,
    sems,
):
    chunks = slot_ref.shape[0]
    dev_rows = SB * TILE_ROWS
    edge = EDGE * TILE_ROWS
    scaling = scale_ref[0] * (1.0 / math.sqrt(table_ref.shape[1]))
    odd = odd_ref[0]
    loads = []
    sides = [(odd, spec_cross, info_cross), (1 - odd, spec_partner, info_partner)]
    for n, (side, spec, info) in enumerate(sides):
        big = pl.ds(pl.multiple_of(side * dev_rows, dev_rows), dev_rows)
        loads += [
            pltpu.make_async_copy(spec, side_ref.at[big], load_sems.at[n, 0]),
            pltpu.make_async_copy(info, info_ref.at[side], load_sems.at[n, 1]),
            pltpu.make_async_copy(info, band_ref.at[side], load_sems.at[n, 2]),
        ]
    for load in loads:
        load.start()
    specs = (side_ref.at[pl.ds(0, dev_rows)], spec_own, side_ref.at[pl.ds(dev_rows, dev_rows)])
    infos = (info_ref.at[0], info_own, info_ref.at[1])
    bands = (band_ref.at[0], band_own, band_ref.at[1])

    def weigh(upper, source):
        pair = table_ref[upper * edge : (upper + 1) * edge, :]
        for k in range(SB):
            column = ((source - upper) * SB + k) * TILE_ROWS
            block = specs[source][k * TILE_ROWS : (k + 1) * TILE_ROWS, :]
            logits = matmul(pair, block, ((1,), (1,)))
            for e in range(EDGE):
                tag = upper * EDGE + e + (EDGE + TILE_DEV * (1 - source) + 1)
                place = jnp.int32(-1)
                for j in range(NB):
                    place = jnp.where(bands[source][SB + k, j] == tag, j, place)
                active = place >= 0
                span = slice(e * TILE_ROWS, (e + 1) * TILE_ROWS)
                weight_ref[upper, span, column : column + TILE_ROWS] = doubled_weights(
                    logits[span, :],
                    jnp.where(active, 0.5 * scaling, 0.0),
                    jnp.where(active, 0.5 * bias_ref[0], -1e30),
                    infos[source][k : k + 1, :],
                    jnp.where(active, place, 2 * NB) * TILE_ROWS,
                )

    def reduce(upper):
        total = matmul(weight_ref[upper, :, :dev_rows], specs[upper][...])
        total += matmul(weight_ref[upper, :, dev_rows:], specs[upper + 1][...])
        grad_ref[upper * edge : (upper + 1) * edge, :] = (0.5 * scaling * total).astype(
            jnp.bfloat16
        )

    weigh(0, 1)
    weigh(1, 1)
    for load in loads:
        load.wait()
    weigh(0, 0)
    reduce(0)
    weigh(1, 2)
    reduce(1)

    def back_step(q, carry):
        for g in range(GROUP):
            columns_onehot(slot_ref[pl.ds(q * GROUP + g, 1), :], mask_ref, g * CHUNK)
        back = matmul(mask_ref[...], grad_ref[...])
        start = pl.multiple_of(q * WIDE, WIDE)
        rows_ref[pl.ds(start, WIDE), :] = back.astype(jnp.bfloat16)
        chunk_copy(rows_ref, back_ref, sems, q).start()
        return carry

    lax.fori_loop(0, chunks // GROUP, back_step, 0)
    for q in range(chunks // GROUP):
        chunk_copy(rows_ref, back_ref, sems, q).wait()


def tiles(scale, bias, odd, table, slot, spectra, info, others):
    rows, width = table.shape
    chunks = slot.shape[0]
    slots = chunks * CHUNK
    return pl.pallas_call(
        tiles_kernel,
        in_specs=[IN_SMEM] * 3 + [IN_VMEM] * 4 + [IN_SMEM] + [ANYWHERE] * 4,
        out_specs=IN_HBM,
        out_shape=pltpu.HBM((slots, width), jnp.bfloat16),
        scratch_shapes=[
            pltpu.VMEM((WIDE, rows), jnp.bfloat16),
            pltpu.VMEM((2, EDGE * TILE_ROWS, 2 * SB * TILE_ROWS), jnp.bfloat16),
            pltpu.VMEM((rows, width), jnp.bfloat16),
            pltpu.VMEM((2 * SB * TILE_ROWS, width), jnp.bfloat16),
            pltpu.VMEM((2, 2 * SB, TILE_ROWS), jnp.int32),
            pltpu.SMEM((2, 2 * SB, TILE_ROWS), jnp.int32),
            pltpu.VMEM((slots, width), jnp.bfloat16),
            pltpu.SemaphoreType.DMA((2, 3)),
            pltpu.SemaphoreType.DMA((chunks // GROUP,)),
        ],
        compiler_params=PARAMS,
        name="tiles",
    )(scale, bias, odd, table, slot, spectra, info, info, *map(in_hbm, others[:2]), *others[2:])


def spectra_kernel(
    scale_ref, bias_ref, odd_ref, band_ref, cross_ref, own_ref, partner_ref, spec_ref, info_ref,
    out_ref, ext_ref, sems,
):
    k = pl.program_id(0)
    edge = EDGE * TILE_ROWS
    scaling = scale_ref[0] * (1.0 / math.sqrt(out_ref.shape[1]))

    @pl.when(k == 0)
    def _():
        mine = TILE_DEV * TILE_ROWS
        low = pl.multiple_of(odd_ref[0] * (edge + mine), edge)
        high = pl.multiple_of(edge + mine - low, edge)
        copies = [
            pltpu.make_async_copy(cross_ref, ext_ref.at[pl.ds(low, edge)], sems.at[0]),
            pltpu.make_async_copy(own_ref, ext_ref.at[pl.ds(edge, mine)], sems.at[1]),
            pltpu.make_async_copy(partner_ref, ext_ref.at[pl.ds(high, edge)], sems.at[2]),
        ]
        for copy in copies:
            copy.start()
        for copy in copies:
            copy.wait()

    total = jnp.zeros(out_ref.shape, jnp.float32)
    for j in range(NB):
        start = pl.multiple_of((band_ref[SB + k, j] - 1) * TILE_ROWS, TILE_ROWS)
        tile = ext_ref[pl.ds(start, TILE_ROWS), :]
        weights = doubled_weights(
            matmul(tile, spec_ref[...], ((1,), (1,))),
            0.5 * scaling,
            0.5 * bias_ref[0],
            info_ref[pl.ds(k, 1), :],
            j * TILE_ROWS,
        )
        total += matmul(weights, tile, ((0,), (0,)))
    out_ref[...] = (0.5 * scaling * total).astype(jnp.bfloat16)


def spectra_gradient(scale, bias, odd, info, cross, table, partner, spectra):
    width = spectra.shape[1]
    edge = EDGE * TILE_ROWS
    return pl.pallas_call(
        spectra_kernel,
        grid=(SB,),
        in_specs=[
            IN_SMEM,
            IN_SMEM,
            IN_SMEM,
            IN_SMEM,
            ANYWHERE,
            ANYWHERE,
            ANYWHERE,
            pl.BlockSpec((TILE_ROWS, width), lambda k: (k, 0)),
            pl.BlockSpec((2 * SB, TILE_ROWS), lambda k: (0, 0)),
        ],
        out_specs=pl.BlockSpec((TILE_ROWS, width), lambda k: (k, 0)),
        scratch_shapes=[
            pltpu.VMEM((4 * edge, width), jnp.bfloat16),
            pltpu.SemaphoreType.DMA((3,)),
        ],
        compiler_params=PARAMS,
        out_shape=jax.ShapeDtypeStruct((SB * TILE_ROWS, width), jnp.bfloat16),
        name="spectra_gradient",
    )(scale, bias, odd, info, cross, table, partner, spectra, info)


def home_kernel(pos_ref, got_ref, out_ref, pick_ref, grad_ref, sems):
    chunks = pos_ref.shape[0]
    for c in range(chunks // GROUP):
        pick = pick_ref.at[c % 2]
        for g in range(GROUP):
            columns_onehot(pos_ref[c * GROUP + g : c * GROUP + g + 1, :], pick, g * CHUNK)
        grad = matmul(pick[...], got_ref[...])
        grad_ref[c * WIDE : (c + 1) * WIDE, :] = grad.astype(jnp.bfloat16)
        chunk_copy(grad_ref, out_ref, sems, c).start()
    for c in range(chunks // GROUP):
        chunk_copy(grad_ref, out_ref, sems, c).wait()


def home(position, returned):
    slots, width = returned.shape
    chunks = position.shape[0]
    rows = chunks * CHUNK
    return pl.pallas_call(
        home_kernel,
        in_specs=[IN_VMEM] * 2,
        out_specs=IN_HBM,
        out_shape=jax.ShapeDtypeStruct((rows, width), jnp.bfloat16),
        scratch_shapes=[
            pltpu.VMEM((2, WIDE, slots), jnp.bfloat16),
            pltpu.VMEM((rows, width), jnp.bfloat16),
            pltpu.SemaphoreType.DMA((chunks,)),
        ],
        compiler_params=PARAMS,
        name="home",
    )(position, returned)


def from_partner(value):
    count = lax.axis_size("mass") * lax.axis_size("prot")
    return lax.ppermute(value, AXES, [(i, i ^ 1) for i in range(count)])


def from_cross(value):
    count = lax.axis_size("mass") * lax.axis_size("prot")
    pairs = [(i, i + 1) for i in range(1, count - 1, 2)]
    return lax.ppermute(value, AXES, pairs + [(j, i) for i, j in pairs])


def program(spectra, peptides, destination, band, positive, logit_scale, logit_bias):
    devices = lax.axis_size("mass") * lax.axis_size("prot")
    rows = peptides.shape[0]
    block = 2 * (rows // devices)

    assert devices % 2 == 0
    odd = (lax.axis_index(AXES) & 1).reshape(1)
    spec_cross = from_cross(spectra)
    spec_partner = from_partner(spectra)
    send, position, info = pack(destination, peptides, positive, band, devices, block)
    info_cross = from_cross(info)
    info_partner = from_partner(info)
    got = lax.all_to_all(send, AXES, 0, 0, tiled=True)
    table, slot, to_cross, to_partner = unpack(odd, got, block)
    cross = from_cross(to_cross)
    partner = from_partner(to_partner)
    back = tiles(
        logit_scale, logit_bias, odd, table, slot, spectra, info,
        (spec_cross, spec_partner, info_cross, info_partner),
    )
    returned = lax.all_to_all(back, AXES, 0, 0, tiled=True)
    spec_grad = spectra_gradient(
        logit_scale, logit_bias, odd, info, cross, table, partner, spectra
    )
    return (spec_grad, home(position, returned))


def solution(mesh):
    in_specs = (
        P(AXES, None),
        P(AXES, None),
        P(AXES),
        P(AXES, None),
        P(AXES),
        P(),
        P(),
    )
    out_specs = (P(AXES, None), P(AXES, None))
    return jax.shard_map(program, mesh=mesh, in_specs=in_specs, out_specs=out_specs, check_vma=False)
```
